32 devices in a mesh: tiles: 16 (over z, y, x), depth: 2 (over core).
Axes of the slice: x: 2, y: 2, z: 4, core: 2. Of those that a mesh axis runs over, the one named last changes fastest.
Arguments:
- momentum: float32 [16, 16, 6300], P('tiles', 'depth'), may hold values from -6 to 6
- tracer: float32 [16, 16, 6300], P('tiles', 'depth'), may hold values from -6 to 6
- mom_diffusivity: float32 [16, 16, 6300], P('tiles', 'depth'), may hold values from 0.02 to 0.2
- tra_diffusivity: float32 [16, 16, 6300], P('tiles', 'depth'), may hold values from 0.02 to 0.2
- mixing: float32 [16, 16, 6300], P('tiles', 'depth'), may hold values from 0.05 to 0.4
- wet_mask: int32 [16, 6300], P('tiles'), may hold values 0 or 1
- neighbours: int32 [16, 4], P('tiles'), may hold values from -1 to 15, as said below
- source_edges: int32 [16, 4], P('tiles'), may hold values from 0 to 3, as said below
- flips: int32 [16, 4], P('tiles'), may hold values from 0 to 1
- mom_cotangent: float32 [16, 16, 6300], P('tiles', 'depth'), may hold values from -6 to 6
- tra_cotangent: float32 [16, 16, 6300], P('tiles', 'depth'), may hold values from -6 to 6
Outputs:
- final_momentum: float32 [16, 16, 6300], P('tiles', 'depth')
- final_tracer: float32 [16, 16, 6300], P('tiles', 'depth')
- grad_momentum: float32 [16, 16, 6300], P('tiles', 'depth')
- grad_tracer: float32 [16, 16, 6300], P('tiles', 'depth')
The draws below stay inside these ranges and needn't reach their ends.
Inputs may be any that keep to these rules, and one draw needn't show every extreme that they name: `neighbours`: the neighbour relation is symmetric, also across the fold seam, where a tile's north edge faces another tile's north edge in reverse order; -1 marks a missing neighbour. `source_edges`: for north and south directions the facing edge is north or south, for east and west directions it is east or west.
All inputs are finite; a program needn't handle non-finite values. No bound on the sum of `wet_mask` on one device may be relied on, other than what follows from the above.
Results may differ from the reference program's by a relative error of at most 0.00002.
Values sent between devices are 32-bit elements; how exact they have to be, the bound alone decides.
A program may use at most 64 MiB of HBM per device.

```python
import math
import jax
import jax.numpy as jnp

NI = 90
NJ = 70
TILES_ALL = 16
LEVELS = 16
CELLS = 6300


grid_columns = 8


def topology(key):
    order = jax.random.permutation(jax.random.fold_in(key, 11), TILES_ALL).astype(jnp.int32)
    position = jnp.zeros((TILES_ALL,), jnp.int32).at[order].set(jnp.arange(TILES_ALL, dtype=jnp.int32))
    column = position % grid_columns
    row = position // grid_columns
    rows_all = TILES_ALL // grid_columns
    at_top = row == rows_all - 1
    at_bottom = row == 0
    north_pos = jnp.where(at_top, row * grid_columns + (grid_columns - 1 - column), position + grid_columns)
    south_pos = jnp.clip(position - grid_columns, 0, TILES_ALL - 1)
    east_pos = row * grid_columns + (column + 1) % grid_columns
    west_pos = row * grid_columns + (column + grid_columns - 1) % grid_columns
    north_pos = jnp.clip(north_pos, 0, TILES_ALL - 1)
    found = jnp.stack([order[north_pos], jnp.where(at_bottom, -1, order[south_pos]), order[east_pos], order[west_pos]], axis=1)
    zeros_col = jnp.zeros((TILES_ALL,), jnp.int32)
    facing_edge = jnp.stack([jnp.where(at_top, 0, 1).astype(jnp.int32), zeros_col, zeros_col + 3, zeros_col + 2], axis=1)
    reversed_flag = jnp.stack([at_top.astype(jnp.int32), zeros_col, zeros_col, zeros_col], axis=1)
    return (found.astype(jnp.int32), facing_edge, reversed_flag)


def draw_neighbours(key, part):
    return topology(key)[0]


def draw_source_edges(key, part):
    return topology(key)[1]


def draw_flips(key, part):
    return topology(key)[2]


def touch_ends(drawn, own_key, smallest, high):
    longest = drawn.shape.index(max(drawn.shape))
    spots = []
    for shift in (0, 1):
        where = [jax.random.randint(jax.random.fold_in(own_key, axis), (), 0, length) for axis, length in enumerate(drawn.shape)]
        where[longest] = (where[longest] + shift) % drawn.shape[longest]
        spots.append(tuple(where))
    return drawn.at[spots[0]].set(smallest).at[spots[1]].set(high)


def level_of(stream_key, shape, pieces, least, high):
    level, own = 1.0, jax.random.fold_in(stream_key, 6)
    for dim, shards_of in pieces:
        heights = jnp.exp(jax.random.uniform(jax.random.fold_in(own, dim), (shards_of,), jnp.float32, least / len(pieces), high / len(pieces)))
        level = level * jnp.repeat(heights, shape[dim] // shards_of).reshape([-1 if axis == dim else 1 for axis in range(len(shape))])
    return level


def bell_draw(key, extent, scale, bound, pieces=(), held_as=jnp.bfloat16):
    loudness = level_of(key, extent, pieces, -0.22, 0.18) if pieces else 1.0
    result = jax.random.normal(key, extent, jnp.float32) * scale * loudness
    return jnp.minimum(jnp.maximum(result, -bound), bound).astype(held_as)


def setup_inputs(seed: int = 0) -> dict:
    streams_of = jax.random.split(jax.random.key(seed), 12)
    return {
        "momentum": bell_draw(streams_of[0], (TILES_ALL, LEVELS, CELLS), 1.0, 6.0, ((0, 16), (1, 2)), jnp.float32),
        "tracer": bell_draw(streams_of[1], (TILES_ALL, LEVELS, CELLS), 1.0, 6.0, ((0, 16), (1, 2)), jnp.float32),
        "mom_diffusivity": jnp.clip(jnp.exp(math.log(0.2) - 2.3025851 * jax.random.uniform(streams_of[2], (TILES_ALL, LEVELS, CELLS), jnp.float32) ** level_of(streams_of[2], (TILES_ALL, LEVELS, CELLS), ((0, 16), (1, 2)), -0.2, 0.2)), 0.02, 0.2),
        "tra_diffusivity": jnp.clip(jnp.exp(math.log(0.2) - 2.3025851 * jax.random.uniform(streams_of[3], (TILES_ALL, LEVELS, CELLS), jnp.float32) ** level_of(streams_of[3], (TILES_ALL, LEVELS, CELLS), ((0, 16), (1, 2)), -0.2, 0.2)), 0.02, 0.2),
        "mixing": jnp.clip(jnp.exp(math.log(0.4) - 2.0794415 * jax.random.uniform(streams_of[4], (TILES_ALL, LEVELS, CELLS), jnp.float32) ** level_of(streams_of[4], (TILES_ALL, LEVELS, CELLS), ((0, 16), (1, 2)), -0.2, 0.2)), 0.05, 0.4),
        "wet_mask": touch_ends((jax.random.randint(streams_of[5], (TILES_ALL, CELLS), 0, 4) < 3).astype(jnp.int32), jax.random.fold_in(streams_of[5], 1), 0, 1),
        "neighbours": draw_neighbours(jax.random.fold_in(streams_of[11], 71), 0),
        "source_edges": draw_source_edges(jax.random.fold_in(streams_of[11], 71), 0),
        "flips": draw_flips(jax.random.fold_in(streams_of[11], 71), 0),
        "mom_cotangent": bell_draw(streams_of[9], (TILES_ALL, LEVELS, CELLS), 1.0, 6.0, ((0, 16), (1, 2)), jnp.float32),
        "tra_cotangent": bell_draw(streams_of[10], (TILES_ALL, LEVELS, CELLS), 1.0, 6.0, ((0, 16), (1, 2)), jnp.float32),
    }


def edges_of(field):
    total = field.shape[-1]
    return jnp.concatenate([field[..., total - NI:], field[..., :NI], field[..., NI - 1::NI], field[..., ::NI]], axis=-1)

def pick_edge(chosen, source, flip, direction):
    if direction < 2:
        strip = jnp.where(source[:, None, None] == 0, chosen[..., :NI], chosen[..., NI:2 * NI])
    else:
        strip = jnp.where(source[:, None, None] == 2, chosen[..., 2 * NI:2 * NI + NJ], chosen[..., 2 * NI + NJ:])
    return jnp.where(flip[:, None, None] == 1, strip[..., ::-1], strip)

def facing(edge_all, neighbours, source_edges, flips):
    strips = []
    for direction in range(4):
        target = neighbours[:, direction]
        row_index = jnp.clip(target, 0, edge_all.shape[0] - 1).astype(jnp.int32)
        chosen = jnp.take(edge_all, row_index, axis=0)
        strip = pick_edge(chosen, source_edges[:, direction], flips[:, direction], direction)
        strips.append(jnp.where((target >= 0)[:, None, None], strip, jnp.zeros_like(strip)))
    return jnp.concatenate(strips, axis=-1)

def shifted_sum(values, halo):
    total = values.shape[-1]
    column = jnp.arange(total) % NI
    north = jnp.concatenate([values[..., NI:], halo[..., :NI]], axis=-1)
    south = jnp.concatenate([halo[..., NI:2 * NI], values[..., :total - NI]], axis=-1)
    east_halo = jnp.repeat(halo[..., 2 * NI:2 * NI + NJ], NI, axis=-1)
    west_halo = jnp.repeat(halo[..., 2 * NI + NJ:], NI, axis=-1)
    east = jnp.where(column == NI - 1, east_halo, jnp.concatenate([values[..., 1:], values[..., :1]], axis=-1))
    west = jnp.where(column == 0, west_halo, jnp.concatenate([values[..., -1:], values[..., :-1]], axis=-1))
    return north + south + east + west

def laplace(field, weighted_halo, wet, wet_halo):
    values = shifted_sum(wet * field, weighted_halo)
    weights = shifted_sum(wet, wet_halo)
    return wet * (values - weights * field)

def vertical(field):
    zeros_level = jnp.zeros_like(field[:, :1])
    above = jnp.concatenate([zeros_level, field[:, :-1]], axis=1)
    below = jnp.concatenate([field[:, 1:], zeros_level], axis=1)
    level_index = jnp.arange(field.shape[1])
    has_above = (level_index > 0).astype(jnp.float32)[None, :, None]
    has_below = (level_index < field.shape[1] - 1).astype(jnp.float32)[None, :, None]
    return has_above * (above - field) + has_below * (below - field)

def reference(momentum, tracer, mom_diffusivity, tra_diffusivity, mixing, wet_mask, neighbours, source_edges, flips, mom_cotangent, tra_cotangent):
    wet = wet_mask[:, None, :].astype(jnp.float32)
    wet_halo = facing(edges_of(wet_mask[:, None, :]), neighbours, source_edges, flips).astype(jnp.float32)
    press_scale = LEVELS ** (-0.5)

    def operator(field):
        halo = facing(edges_of(field), neighbours, source_edges, flips)
        return laplace(field, wet_halo * halo, wet, wet_halo)

    def forward_step(state):
        mom_now, tra_now = state
        press = press_scale * jnp.cumsum(tra_now, axis=1)
        mom_next = mom_now + mom_diffusivity * operator(mom_now) - 0.1 * operator(press)
        tra_next = tra_now + tra_diffusivity * operator(tra_now) + mixing * vertical(tra_now) + 0.2 * mom_now
        return (mom_next, tra_next)

    def two_steps(mom_start, tra_start):
        return forward_step(forward_step((mom_start, tra_start)))
    finals, pullback = jax.vjp(two_steps, momentum, tracer)
    grads = pullback((mom_cotangent, tra_cotangent))
    return (finals[0], finals[1], grads[0], grads[1])
```

```python
import functools

import jax
import jax.numpy as jnp
from jax import lax
from jax.experimental import pallas as pl
from jax.experimental.pallas import tpu as pltpu
from jax.sharding import PartitionSpec as P

NI = 90
NJ = 70
CELLS = NI * NJ
LANES = 128
LO = LANES
HI = LANES + CELLS
WIDTH = -(-(HI + NI) // LANES) * LANES
CHUNKS = WIDTH // LANES
FIRST = 64 * NI // LANES
MESH = pl.DeviceIdType.MESH
EXACT = lax.Precision.HIGHEST


def roll(x, shift, axis=1):
    return pltpu.roll(x, shift % x.shape[axis], axis)


def kernel(
    inner, outer, depth, levels_all,
    mom_ref, tra_ref, mdif_ref, tdif_ref, mix_ref, wet_ref, nb_ref, se_ref, fl_ref, mcot_ref, tcot_ref,
    mom_out, tra_out, mgrad_out, tgrad_out,
    table, tables, tables_s, grid, gath_0, gath_1, part, halo, edge_s, edge_r, carry_s, carry_r,
    tab_send, tab_recv, tab_local, g_send, g_recv, h_send, h_recv, e_send, e_recv, c_send, c_recv,
):
    me = lax.axis_index("tiles")
    d = lax.axis_index("depth")
    member = lax.rem(me, inner)
    group = lax.div(me, inner)
    rows = mom_ref.shape[1]
    total = grid.shape[0]
    press = -0.1 * levels_all ** (-0.5)

    def in_inner(o):
        return {"tiles": group * inner + lax.rem(member + o, inner), "depth": d}

    def in_outer(o):
        return {"tiles": lax.rem(group + o, outer) * inner + member, "depth": d}

    def in_depth(o):
        return {"tiles": me, "depth": lax.rem(d + o, depth)}

    barrier = pltpu.get_barrier_semaphore()
    for count, where_to in ((inner, in_inner), (outer, in_outer), (depth, in_depth)):
        for o in range(1, count):
            pl.semaphore_signal(barrier, inc=1, device_id=where_to(o), device_id_type=MESH)
    pl.semaphore_wait(barrier, inner + outer + depth - 3)

    started = []

    def send(src, dst, ssem, rsem, to):
        copy = pltpu.make_async_remote_copy(
            src_ref=src, dst_ref=dst, send_sem=ssem, recv_sem=rsem, device_id=to, device_id_type=MESH
        )
        copy.start()
        started.append(copy)
        return copy

    table[...] = jnp.zeros_like(table)
    table[0:1, 0:4] = nb_ref[...]
    table[1:2, 0:4] = se_ref[...]
    table[2:3, 0:4] = fl_ref[...]
    tables[group] = table[...]
    table_copies = [
        send(table, tables.at[group], tab_send.at[o], tab_recv.at[o], in_outer(o)) for o in range(1, outer)
    ]

    pos = (lax.broadcasted_iota(jnp.int32, (8, WIDTH), 1) - LO).astype(jnp.float32)
    col = pos - NI * jnp.floor((pos + 0.5) * (1.0 / NI))
    inside = (pos > -0.5) & (pos < CELLS - 0.5)
    at_west = (col < 0.5) & inside
    at_east = (col > NI - 1.5) & inside
    on_edge = jnp.where(at_west | at_east, 1.0, 0.0)
    lane = lax.broadcasted_iota(jnp.int32, (total, LANES), 1)
    odd = lax.rem(lane, 2) == 1
    level = lax.broadcasted_iota(jnp.int32, (rows, CELLS), 0)

    r0 = lax.broadcasted_iota(jnp.int32, (LANES, LANES), 0)
    r1 = lax.broadcasted_iota(jnp.int32, (LANES, LANES), 1)
    rev_i = jnp.where(r0 + r1 == NI - 1, 1.0, 0.0)

    wet = jnp.broadcast_to(wet_ref[...].astype(jnp.float32), (rows, CELLS))
    mdif, tdif, mix = mdif_ref[0], tdif_ref[0], mix_ref[0]

    def running(x, down):
        k = 1
        while k < rows:
            if down:
                x = x + jnp.where(level >= k, roll(x, k, 0), 0.0)
            else:
                x = x + jnp.where(level < rows - k, roll(x, rows - k, 0), 0.0)
            k *= 2
        return x

    grid[...] = jnp.zeros_like(grid)
    m, s, lm, lt = mom_ref[0], tra_ref[0], mcot_ref[0], tcot_ref[0]
    has_above = jnp.where(d > 0, 1.0, 0.0)
    has_below = jnp.where(d < depth - 1, 1.0, 0.0)
    weights = None

    for r in range(2):
        gath = (gath_0, gath_1)[r]
        mixed = mix * lt
        edge_copies = []
        if depth > 1:
            edge_s[r, 0, 0:1] = s[rows - 1 : rows]
            edge_s[r, 0, 1:2] = mixed[rows - 1 : rows]
            edge_s[r, 1, 0:1] = s[0:1]
            edge_s[r, 1, 1:2] = mixed[0:1]
            for i, o in ((0, 1), (1, depth - 1)):
                edge_copies.append(
                    send(edge_s.at[r, i], edge_r.at[r, i], e_send.at[r, i], e_recv.at[r, i], in_depth(o))
                )
        back = running(lm, False)
        u = tdif * lt + press * back
        w_m = mdif * lm
        t_sum = press * back[0:1]
        grid[0:rows, LO:HI] = wet * m
        grid[rows : 2 * rows, LO:HI] = wet * s
        grid[2 * rows : 3 * rows, LO:HI] = wet * w_m
        grid[3 * rows : 4 * rows, LO:HI] = wet * u
        grid[4 * rows : 5 * rows, LO:HI] = jnp.where(level == 0, wet, jnp.where(level == 1, wet * t_sum, 0.0))

        gath[member, 0] = roll(grid[:, WIDTH - 2 * LANES : WIDTH], -(HI - NI - (WIDTH - 2 * LANES)))[:, :LANES]
        gath[member, 1] = grid[:, LO : LO + LANES]
        for g in range(5):
            span = slice(g * rows, (g + 1) * rows)
            for part_of, (a, b) in enumerate(((1, 1 + FIRST), (1 + FIRST, CHUNKS))):
                acc = None
                for v in range(a, b):
                    cut = slice(v * LANES, (v + 1) * LANES)
                    piece = grid[span, cut] * on_edge[:, cut]
                    acc = piece if acc is None else acc + piece
                gath[member, 2 + part_of, span] = acc
        copies = [
            send(gath.at[member], gath.at[member], g_send.at[r, o], g_recv.at[r, o], in_inner(o))
            for o in range(1, inner)
        ]
        if r == 0:
            for copy in table_copies:
                copy.wait_recv()
            local = pltpu.make_async_copy(tables, tables_s, tab_local)
            local.start()
            local.wait()
        for copy in copies:
            copy.wait_recv()

        def strips_for(target):
            def source(direction):
                tile = tables_s[target, 0, direction]
                edge = tables_s[target, 1, direction]
                known = jnp.maximum(tile, 0)
                here = (tile >= 0) & (lax.div(known, inner) == group)
                return lax.rem(known, inner), edge, jnp.where(here, 1.0, 0.0)

            result = []
            for direction in range(2):
                tile, edge, here = source(direction)
                result.append(gath[tile, jnp.where(edge == 0, 0, 1)] * here)
            east, east_edge, east_here = source(2)
            west, west_edge, west_here = source(3)
            east_turn = jnp.where(east_edge == 3, 1.0, 0.0)
            west_turn = jnp.where(west_edge == 2, 1.0, 0.0)
            for k in (2, 3):
                e = gath[east, k]
                e = (roll(e, NI - 1) * east_turn + e * (1.0 - east_turn)) * east_here
                w = gath[west, k]
                w = (roll(w, 1 - NI) * west_turn + w * (1.0 - west_turn)) * west_here
                result.append(jnp.where(odd, e, w))
            return result

        copies = []
        for o in range(1, outer):
            for k, strip in enumerate(strips_for(lax.rem(group + o, outer))):
                part[r, o, k] = strip
            copies.append(send(part.at[r, o], halo.at[r, o], h_send.at[r, o], h_recv.at[r, o], in_outer(o)))
        strips = strips_for(group)
        for o in range(1, outer):
            copies[o - 1].wait_recv()
            for k in range(4):
                strips[k] = strips[k] + halo[r, o, k]

        flip = [jnp.where(tables_s[group, 2, k] == 1, 1.0, 0.0) for k in range(4)]
        dot = functools.partial(jnp.dot, precision=EXACT, preferred_element_type=jnp.float32)
        north = dot(strips[0], rev_i) * flip[0] + strips[0] * (1.0 - flip[0])
        south = dot(strips[1], rev_i) * flip[1] + strips[1] * (1.0 - flip[1])
        both = lax.rem(r0, 2) == 0
        aim = jnp.where(both, NI * (NJ - 1) % LANES, (NI * (NJ - 1) + 2 * (NI - 1)) % LANES)
        turn = jnp.where(lax.rem(r0 + r1 + LANES * 4 - aim, LANES) == 0, 1.0, 0.0)
        one, two = dot(strips[2], turn), dot(strips[3], turn)
        tail = jnp.zeros((total, LANES), jnp.float32)
        for j in range(NJ - 64):
            for x in (NI * j % LANES, (NI * j + NI - 1) % LANES):
                tail = jnp.where(lane == x, 1.0, tail)
        turned_one = jnp.where(tail > 0.5, two, one)
        turned_two = jnp.where(tail > 0.5, one, 0.0)
        ew_flip = jnp.where(odd, flip[2], flip[3])
        ew_one = jnp.where(ew_flip > 0.5, turned_one, strips[2])
        ew_two = jnp.where(ew_flip > 0.5, turned_two, strips[3])

        grid[:, 0:LANES] = roll(south, LANES - NI)
        end = WIDTH - LANES
        grid[:, end:] = jnp.where(lane < HI - end, grid[:, end:], roll(north, HI - end))

        def around(g):
            span = slice(g * rows, (g + 1) * rows)
            x = grid[span, :]
            side = jnp.concatenate(
                [ew_one[span]] * (1 + FIRST) + [ew_two[span]] * (CHUNKS - 1 - FIRST), axis=1
            )
            east = jnp.where(at_east, side, roll(x, -1))
            west = jnp.where(at_west, side, roll(x, 1))
            return (roll(x, -NI) + roll(x, NI) + east + west)[:, LO:HI]

        extra = around(4)
        weights = extra[0:1]
        lap_t = wet[0:1] * (extra[1:2] - weights * t_sum)
        lap_s = wet * (around(1) - weights * s)
        sums = running(lap_s, True)
        copies = []
        if depth > 1:
            carry_s[r, 0:1] = sums[rows - 1 : rows]
            carry_s[r, 1:2] = lap_t
            copies = [
                send(carry_s.at[r], carry_r.at[r, o], c_send.at[r, o], c_recv.at[r, o], in_depth(o))
                for o in range(1, depth)
            ]
        lap_m = wet * (around(0) - weights * m)
        lap_w = wet * (around(2) - weights * w_m)
        lap_u = wet * (around(3) - weights * u)
        m_next = m + mdif * lap_m + press * sums
        lm_next = lm + lap_w + 0.2 * lt

        for copy in edge_copies:
            copy.wait_recv()

        def vertical(q, which):
            above, below = q[0:1], q[rows - 1 : rows]
            if depth > 1:
                above = edge_r[r, 0, which : which + 1] * has_above + above * (1.0 - has_above)
                below = edge_r[r, 1, which : which + 1] * has_below + below * (1.0 - has_below)
            up = jnp.where(level == 0, above, roll(q, 1, 0))
            down = jnp.where(level == rows - 1, below, roll(q, rows - 1, 0))
            return (up - q) + (down - q)

        s_next = s + tdif * lap_s + mix * vertical(s, 0) + 0.2 * m
        lt_next = lt + lap_u + vertical(mixed, 1)
        for o in range(1, depth):
            copies[o - 1].wait_recv()
            origin = lax.rem(d + depth - o, depth)
            m_next = m_next + carry_r[r, o, 0:1] * jnp.where(origin < d, press, 0.0)
            lt_next = lt_next + carry_r[r, o, 1:2] * jnp.where(origin > d, 1.0, 0.0)
        m, s, lm, lt = m_next, s_next, lm_next, lt_next

    mom_out[0] = m
    tra_out[0] = s
    mgrad_out[0] = lm
    tgrad_out[0] = lt
    for copy in started:
        copy.wait_send()


def solution(mesh):
    tiles, depth = mesh.shape["tiles"], mesh.shape["depth"]
    inner = max(k for k in range(1, tiles + 1) if tiles % k == 0 and k * k <= tiles)
    outer = tiles // inner

    def local(*args):
        rows = args[0].shape[1]
        total = 5 * rows
        dma = pltpu.SemaphoreType.DMA
        f32 = jnp.float32
        shape = jax.ShapeDtypeStruct(args[0].shape, f32)
        vmem = pl.BlockSpec(memory_space=pltpu.VMEM)
        return pl.pallas_call(
            functools.partial(kernel, inner, outer, depth, rows * depth),
            out_shape=(shape,) * 4,
            in_specs=[vmem] * 11,
            out_specs=(vmem,) * 4,
            scratch_shapes=[
                pltpu.VMEM((8, LANES), jnp.int32),
                pltpu.VMEM((outer, 8, LANES), jnp.int32),
                pltpu.SMEM((outer, 8, LANES), jnp.int32),
                pltpu.VMEM((total, WIDTH), f32),
                pltpu.VMEM((inner, 4, total, LANES), f32),
                pltpu.VMEM((inner, 4, total, LANES), f32),
                pltpu.VMEM((2, outer, 4, total, LANES), f32),
                pltpu.VMEM((2, outer, 4, total, LANES), f32),
                pltpu.VMEM((2, 2, 2, CELLS), f32),
                pltpu.VMEM((2, 2, 2, CELLS), f32),
                pltpu.VMEM((2, 2, CELLS), f32),
                pltpu.VMEM((2, depth, 2, CELLS), f32),
                dma((outer,)), dma((outer,)), dma(()),
                dma((2, inner)), dma((2, inner)),
                dma((2, outer)), dma((2, outer)),
                dma((2, 2)), dma((2, 2)),
                dma((2, depth)), dma((2, depth)),
            ],
            compiler_params=pltpu.CompilerParams(
                collective_id=0, has_side_effects=True, vmem_limit_bytes=48 * 1024 * 1024
            ),
        )(*args)

    whole = P("tiles", "depth", None)
    flat = P("tiles", None)
    in_specs = (whole,) * 5 + (flat,) * 4 + (whole,) * 2
    return jax.shard_map(local, mesh=mesh, in_specs=in_specs, out_specs=(whole,) * 4, check_vma=False)
```

```python
import functools

import jax
import jax.numpy as jnp
from jax import lax
from jax.experimental import pallas as pl
from jax.experimental.pallas import tpu as pltpu
from jax.sharding import PartitionSpec as P

NI = 90
NJ = 70
CELLS = NI * NJ
LANES = 128
LO = LANES
HI = LANES + CELLS
WIDTH = -(-(HI + NI) // LANES) * LANES
CHUNKS = WIDTH // LANES
FIRST = 64 * NI // LANES
MESH = pl.DeviceIdType.MESH
EXACT = lax.Precision.HIGHEST


def roll(x, shift, axis=1):
    return pltpu.roll(x, shift % x.shape[axis], axis)


def kernel(
    inner, outer, depth, levels_all,
    mom_hbm, tra_hbm, mdif_hbm, tdif_hbm, mix_hbm, wet_hbm, nb_hbm, se_hbm, fl_hbm, mcot_hbm, tcot_hbm,
    mom_out, tra_out, mgrad_out, tgrad_out,
    mom_ref, tra_ref, mdif_ref, tdif_ref, mix_ref, wet_ref, nb_ref, se_ref, fl_ref, mcot_ref, tcot_ref,
    table, tables, tables_s, grid, gath_0, gath_1, part, halo, edge_s, edge_r, carry_s, carry_r,
    in_sem, tab_send, tab_recv, tab_local, g_send, g_recv, h_send, h_recv, e_send, e_recv, c_send, c_recv,
):
    me = lax.axis_index("tiles")
    d = lax.axis_index("depth")
    member = lax.rem(me, inner)
    group = lax.div(me, inner)
    rows = mom_ref.shape[1]
    total = grid.shape[0]
    press = -0.1 * levels_all ** (-0.5)

    def in_inner(o):
        return {"tiles": group * inner + lax.rem(member + o, inner), "depth": d}

    def in_outer(o):
        return {"tiles": lax.rem(group + o, outer) * inner + member, "depth": d}

    def in_depth(o):
        return {"tiles": me, "depth": lax.rem(d + o, depth)}

    fetched = []
    for k, (src, dst) in enumerate((
        (nb_hbm, nb_ref), (se_hbm, se_ref), (fl_hbm, fl_ref), (wet_hbm, wet_ref), (mcot_hbm, mcot_ref),
        (tdif_hbm, tdif_ref), (tcot_hbm, tcot_ref), (tra_hbm, tra_ref), (mom_hbm, mom_ref), (mdif_hbm, mdif_ref),
        (mix_hbm, mix_ref),
    )):
        fetched.append(pltpu.make_async_copy(src, dst, in_sem.at[k]))
        fetched[-1].start()
    grid[...] = jnp.zeros_like(grid)
    barrier = pltpu.get_barrier_semaphore()
    for count, where_to in ((inner, in_inner), (outer, in_outer), (depth, in_depth)):
        for o in range(1, count):
            pl.semaphore_signal(barrier, inc=1, device_id=where_to(o), device_id_type=MESH)
    pl.semaphore_wait(barrier, inner + outer + depth - 3)

    started = []

    def send(src, dst, ssem, rsem, to):
        copy = pltpu.make_async_remote_copy(
            src_ref=src, dst_ref=dst, send_sem=ssem, recv_sem=rsem, device_id=to, device_id_type=MESH
        )
        copy.start()
        started.append(copy)
        return copy

    for copy in fetched[:3]:
        copy.wait()
    table[...] = jnp.zeros_like(table)
    table[0:1, 0:4] = nb_ref[...]
    table[1:2, 0:4] = se_ref[...]
    table[2:3, 0:4] = fl_ref[...]
    tables[group] = table[...]
    table_copies = [
        send(table, tables.at[group], tab_send.at[o], tab_recv.at[o], in_outer(o)) for o in range(1, outer)
    ]

    pos = (lax.broadcasted_iota(jnp.int32, (8, WIDTH), 1) - LO).astype(jnp.float32)
    col = pos - NI * jnp.floor((pos + 0.5) * (1.0 / NI))
    inside = (pos > -0.5) & (pos < CELLS - 0.5)
    at_west = (col < 0.5) & inside
    at_east = (col > NI - 1.5) & inside
    on_edge = jnp.where(at_west | at_east, 1.0, 0.0)
    lane = lax.broadcasted_iota(jnp.int32, (total, LANES), 1)
    odd = lax.rem(lane, 2) == 1
    odd6 = lax.rem(lax.broadcasted_iota(jnp.int32, (6 * rows, LANES), 1), 2) == 1
    level = lax.broadcasted_iota(jnp.int32, (rows, CELLS), 0)
    level8 = lax.broadcasted_iota(jnp.int32, (rows, LANES), 0)
    tail = jnp.zeros((total, LANES), jnp.float32)
    for j in range(NJ - 64):
        for x in (NI * j % LANES, (NI * j + NI - 1) % LANES):
            tail = jnp.where(lane == x, 1.0, tail)

    r0 = lax.broadcasted_iota(jnp.int32, (LANES, LANES), 0)
    r1 = lax.broadcasted_iota(jnp.int32, (LANES, LANES), 1)
    rev_i = jnp.where(r0 + r1 == NI - 1, 1.0, 0.0)

    for copy in fetched[3:]:
        copy.wait()
    wet = jnp.broadcast_to(wet_ref[...].astype(jnp.float32), (rows, CELLS))
    mdif, tdif, mix = mdif_ref[0], tdif_ref[0], mix_ref[0]

    def running(x, down):
        k = 1
        while k < rows:
            if down:
                x = x + jnp.where(level >= k, roll(x, k, 0), 0.0)
            else:
                x = x + jnp.where(level < rows - k, roll(x, rows - k, 0), 0.0)
            k *= 2
        return x

    m, s, lm, lt = mom_ref[0], tra_ref[0], mcot_ref[0], tcot_ref[0]
    has_above = jnp.where(d > 0, 1.0, 0.0)
    has_below = jnp.where(d < depth - 1, 1.0, 0.0)
    weights = None

    for r in range(2):
        gath = (gath_0, gath_1)[r]
        mixed = mix * lt
        edge_copies = []
        if depth > 1:
            edge_s[r, 0, 0:1] = s[rows - 1 : rows]
            edge_s[r, 0, 1:2] = mixed[rows - 1 : rows]
            edge_s[r, 1, 0:1] = s[0:1]
            edge_s[r, 1, 1:2] = mixed[0:1]
            for i, o in ((0, 1), (1, depth - 1)):
                edge_copies.append(
                    send(edge_s.at[r, i], edge_r.at[r, i], e_send.at[r, i], e_recv.at[r, i], in_depth(o))
                )
        back = running(lm, False)
        u = tdif * lt + press * back
        w_m = mdif * lm
        t_sum = press * back[0:1]
        grid[0:rows, LO:HI] = wet * m
        grid[rows : 2 * rows, LO:HI] = wet * s
        grid[2 * rows : 3 * rows, LO:HI] = wet * w_m
        grid[3 * rows : 4 * rows, LO:HI] = wet * u
        grid[4 * rows : 5 * rows, LO:HI] = jnp.where(level == 0, wet, jnp.where(level == 1, wet * t_sum, 0.0))

        tail_at = WIDTH - 2 * LANES
        north = roll(grid[:, tail_at:WIDTH], -(HI - NI - tail_at))[:, :LANES]
        south = grid[:, LO : LO + LANES]
        last = None
        for g in range(5):
            span = slice(g * rows, (g + 1) * rows)
            packed = []
            for a, b in ((1, 1 + FIRST), (1 + FIRST, CHUNKS)):
                acc = None
                for v in range(a, b):
                    cut = slice(v * LANES, (v + 1) * LANES)
                    piece = grid[span, cut] * on_edge[:, cut]
                    acc = piece if acc is None else acc + piece
                packed.append(acc)
            last = packed[1] if g == 0 else last + roll(packed[1], 2 * g)
            if g < 4:
                gath[member, g] = north[span]
                gath[member, 4 + g] = south[span]
                gath[member, 8 + g] = packed[0]
            else:
                gath[member, 12] = jnp.where(level8 < 2, north[span], 0.0) + roll(
                    jnp.where(level8 < 2, south[span], 0.0), 2, 0
                ) + roll(packed[0], 4, 0)
        gath[member, 13] = last
        copies = [
            send(gath.at[member], gath.at[member], g_send.at[r, o], g_recv.at[r, o], in_inner(o))
            for o in range(1, inner)
        ]
        if r == 0:
            for copy in table_copies:
                copy.wait_recv()
            local = pltpu.make_async_copy(tables, tables_s, tab_local)
            local.start()
            local.wait()
        for copy in copies:
            copy.wait_recv()

        def strips_for(target):
            def source(direction):
                tile = tables_s[target, 0, direction]
                edge = tables_s[target, 1, direction]
                known = jnp.maximum(tile, 0)
                here = (tile >= 0) & (lax.div(known, inner) == group)
                return lax.rem(known, inner), edge, jnp.where(here, 1.0, 0.0)

            result = []
            odds = []
            for direction in range(2):
                tile, edge, here = source(direction)
                edge = jnp.where(edge == 0, 0, 1)
                result.append((gath[tile, pl.ds(4 * edge, 4)] * here).reshape(4 * rows, LANES))
                two = gath[tile, 12] * here
                second = edge.astype(jnp.float32)
                odds.append(roll(two, -2, 0) * second + two * (1.0 - second))
            east, east_edge, east_here = source(2)
            west, west_edge, west_here = source(3)
            east_turn = jnp.where(east_edge == 3, 1.0, 0.0)
            west_turn = jnp.where(west_edge == 2, 1.0, 0.0)
            e = gath[east, 8:14].reshape(6 * rows, LANES)
            e = (roll(e, NI - 1) * east_turn + e * (1.0 - east_turn)) * east_here
            w = gath[west, 8:14].reshape(6 * rows, LANES)
            w = (roll(w, 1 - NI) * west_turn + w * (1.0 - west_turn)) * west_here
            side = jnp.where(odd6, e, w)
            mid = side[4 * rows : 5 * rows]
            mid = jnp.where(level8 < 2, odds[0], jnp.where(level8 < 4, roll(odds[1], 2, 0), mid))
            return jnp.concatenate([result[0], result[1], side[: 4 * rows], mid, side[5 * rows :]], axis=0)

        copies = []
        for o in range(1, outer):
            part[r, o] = strips_for(lax.rem(group + o, outer)).reshape(14, rows, LANES)
            copies.append(send(part.at[r, o], halo.at[r, o], h_send.at[r, o], h_recv.at[r, o], in_outer(o)))
        merged = strips_for(group)
        for o in range(1, outer):
            copies[o - 1].wait_recv()
            merged = merged + halo[r, o].reshape(14 * rows, LANES)
        mid, last = merged[12 * rows : 13 * rows], merged[13 * rows :]
        strips = [
            jnp.concatenate([merged[: 4 * rows], mid], axis=0),
            jnp.concatenate([merged[4 * rows : 8 * rows], roll(mid, -2, 0)], axis=0),
            jnp.concatenate([merged[8 * rows : 12 * rows], roll(mid, -4, 0)], axis=0),
            jnp.where(tail > 0.5, jnp.concatenate([roll(last, -2 * g) for g in range(5)], axis=0), 0.0),
        ]

        flip = [jnp.where(tables_s[group, 2, k] == 1, 1.0, 0.0) for k in range(4)]
        dot = functools.partial(jnp.dot, precision=EXACT, preferred_element_type=jnp.float32)
        north = dot(strips[0], rev_i) * flip[0] + strips[0] * (1.0 - flip[0])
        south = dot(strips[1], rev_i) * flip[1] + strips[1] * (1.0 - flip[1])
        both = lax.rem(r0, 2) == 0
        aim = jnp.where(both, NI * (NJ - 1) % LANES, (NI * (NJ - 1) + 2 * (NI - 1)) % LANES)
        turn = jnp.where(lax.rem(r0 + r1 + LANES * 4 - aim, LANES) == 0, 1.0, 0.0)
        one, two = dot(strips[2], turn), dot(strips[3], turn)
        turned_one = jnp.where(tail > 0.5, two, one)
        turned_two = jnp.where(tail > 0.5, one, 0.0)
        ew_flip = jnp.where(odd, flip[2], flip[3])
        ew_one = jnp.where(ew_flip > 0.5, turned_one, strips[2])
        ew_two = jnp.where(ew_flip > 0.5, turned_two, strips[3])

        grid[:, 0:LANES] = roll(south, LANES - NI)
        end = WIDTH - LANES
        grid[:, end:] = jnp.where(lane < HI - end, grid[:, end:], roll(north, HI - end))

        def around(g):
            span = slice(g * rows, (g + 1) * rows)
            x = grid[span, :]
            side = jnp.concatenate(
                [ew_one[span]] * (1 + FIRST) + [ew_two[span]] * (CHUNKS - 1 - FIRST), axis=1
            )
            east = jnp.where(at_east, side, roll(x, -1))
            west = jnp.where(at_west, side, roll(x, 1))
            return (roll(x, -NI) + roll(x, NI) + east + west)[:, LO:HI]

        extra = around(4)
        weights = extra[0:1]
        lap_t = wet[0:1] * (extra[1:2] - weights * t_sum)
        lap_s = wet * (around(1) - weights * s)
        sums = running(lap_s, True)
        copies = []
        if depth > 1:
            carry_s[r, 0:1] = sums[rows - 1 : rows]
            carry_s[r, 1:2] = lap_t
            copies = [
                send(carry_s.at[r], carry_r.at[r, o], c_send.at[r, o], c_recv.at[r, o], in_depth(o))
                for o in range(1, depth)
            ]
        lap_m = wet * (around(0) - weights * m)
        lap_w = wet * (around(2) - weights * w_m)
        lap_u = wet * (around(3) - weights * u)
        m_next = m + mdif * lap_m + press * sums
        lm_next = lm + lap_w + 0.2 * lt

        for copy in edge_copies:
            copy.wait_recv()

        def vertical(q, which):
            above, below = q[0:1], q[rows - 1 : rows]
            if depth > 1:
                above = edge_r[r, 0, which : which + 1] * has_above + above * (1.0 - has_above)
                below = edge_r[r, 1, which : which + 1] * has_below + below * (1.0 - has_below)
            up = jnp.where(level == 0, above, roll(q, 1, 0))
            down = jnp.where(level == rows - 1, below, roll(q, rows - 1, 0))
            return (up - q) + (down - q)

        s_next = s + tdif * lap_s + mix * vertical(s, 0) + 0.2 * m
        lt_next = lt + lap_u + vertical(mixed, 1)
        for o in range(1, depth):
            copies[o - 1].wait_recv()
            origin = lax.rem(d + depth - o, depth)
            m_next = m_next + carry_r[r, o, 0:1] * jnp.where(origin < d, press, 0.0)
            lt_next = lt_next + carry_r[r, o, 1:2] * jnp.where(origin > d, 1.0, 0.0)
        m, s, lm, lt = m_next, s_next, lm_next, lt_next

    mom_out[0] = m
    tra_out[0] = s
    mgrad_out[0] = lm
    tgrad_out[0] = lt
    for copy in started:
        copy.wait_send()


def write_out(*refs):
    sems = refs[8]
    copies = [pltpu.make_async_copy(refs[k], refs[4 + k], sems.at[k]) for k in range(4)]
    for copy in copies:
        copy.start()
    for copy in copies:
        copy.wait()


def solution(mesh):
    tiles, depth = mesh.shape["tiles"], mesh.shape["depth"]
    inner = max(k for k in range(1, tiles + 1) if tiles % k == 0 and k * k <= tiles)
    outer = tiles // inner

    def local(*args):
        rows = args[0].shape[1]
        total = 5 * rows
        dma = pltpu.SemaphoreType.DMA
        f32 = jnp.float32
        shape = jax.ShapeDtypeStruct(args[0].shape, f32)
        vmem = pl.BlockSpec(memory_space=pltpu.VMEM)
        hbm = pl.BlockSpec(memory_space=pltpu.MemorySpace.HBM)
        results = pl.pallas_call(
            functools.partial(kernel, inner, outer, depth, rows * depth),
            out_shape=(shape,) * 4,
            in_specs=[hbm] * 11,
            out_specs=(vmem,) * 4,
            scratch_shapes=[
                *[pltpu.VMEM(a.shape, a.dtype) for a in args],
                pltpu.VMEM((8, LANES), jnp.int32),
                pltpu.VMEM((outer, 8, LANES), jnp.int32),
                pltpu.SMEM((outer, 8, LANES), jnp.int32),
                pltpu.VMEM((total, WIDTH), f32),
                pltpu.VMEM((inner, 14, rows, LANES), f32),
                pltpu.VMEM((inner, 14, rows, LANES), f32),
                pltpu.VMEM((2, outer, 14, rows, LANES), f32),
                pltpu.VMEM((2, outer, 14, rows, LANES), f32),
                pltpu.VMEM((2, 2, 2, CELLS), f32),
                pltpu.VMEM((2, 2, 2, CELLS), f32),
                pltpu.VMEM((2, 2, CELLS), f32),
                pltpu.VMEM((2, depth, 2, CELLS), f32),
                dma((11,)), dma((outer,)), dma((outer,)), dma(()),
                dma((2, inner)), dma((2, inner)),
                dma((2, outer)), dma((2, outer)),
                dma((2, 2)), dma((2, 2)),
                dma((2, depth)), dma((2, depth)),
            ],
            compiler_params=pltpu.CompilerParams(
                collective_id=0, has_side_effects=True, vmem_limit_bytes=62 * 1024 * 1024
            ),
        )(*args)
        return pl.pallas_call(
            write_out,
            out_shape=(shape,) * 4,
            in_specs=[pl.BlockSpec(memory_space=pl.ANY)] * 4,
            out_specs=(hbm,) * 4,
            scratch_shapes=[dma((4,))],
        )(*results)

    whole = P("tiles", "depth", None)
    flat = P("tiles", None)
    in_specs = (whole,) * 5 + (flat,) * 4 + (whole,) * 2
    return jax.shard_map(local, mesh=mesh, in_specs=in_specs, out_specs=(whole,) * 4, check_vma=False)
```

```python
import functools

import jax
import jax.numpy as jnp
from jax import lax
from jax.experimental import pallas as pl
from jax.experimental.pallas import tpu as pltpu
from jax.sharding import PartitionSpec as P

NI = 90
NJ = 70
CELLS = NI * NJ
LANES = 128
LO = LANES
HI = LANES + CELLS
WIDTH = -(-(HI + NI) // LANES) * LANES
CHUNKS = WIDTH // LANES
FIRST = 64 * NI // LANES
MESH = pl.DeviceIdType.MESH
EXACT = lax.Precision.HIGHEST


def roll(x, shift, axis=1):
    return pltpu.roll(x, shift % x.shape[axis], axis)


def kernel(
    inner, outer, depth, levels_all,
    mom_hbm, tra_hbm, mdif_hbm, tdif_hbm, mix_hbm, wet_hbm, nb_hbm, se_hbm, fl_hbm, mcot_hbm, tcot_hbm,
    mom_out, tra_out, mgrad_out, tgrad_out,
    mom_ref, tra_ref, mdif_ref, tdif_ref, mix_ref, wet_ref, nb_ref, se_ref, fl_ref, mcot_ref, tcot_ref,
    table, tables, tables_s, grid, gath_0, gath_1, part, halo, edge_s, edge_r, carry_s, carry_r,
    in_sem, tab_send, tab_recv, tab_local, g_send, g_recv, h_send, h_recv, e_send, e_recv, c_send, c_recv,
):
    me = lax.axis_index("tiles")
    d = lax.axis_index("depth")
    member = lax.rem(me, inner)
    group = lax.div(me, inner)
    rows = mom_ref.shape[1]
    total = grid.shape[0]
    press = -0.1 * levels_all ** (-0.5)

    def in_inner(o):
        return {"tiles": group * inner + lax.rem(member + o, inner), "depth": d}

    def in_outer(o):
        return {"tiles": lax.rem(group + o, outer) * inner + member, "depth": d}

    def in_depth(o):
        return {"tiles": me, "depth": lax.rem(d + o, depth)}

    fetched = []
    for k, (src, dst) in enumerate((
        (nb_hbm, nb_ref), (se_hbm, se_ref), (fl_hbm, fl_ref), (wet_hbm, wet_ref), (mcot_hbm, mcot_ref),
        (tdif_hbm, tdif_ref), (tcot_hbm, tcot_ref), (tra_hbm, tra_ref), (mom_hbm, mom_ref), (mdif_hbm, mdif_ref),
        (mix_hbm, mix_ref),
    )):
        fetched.append(pltpu.make_async_copy(src, dst, in_sem.at[k]))
        fetched[-1].start()
    grid[...] = jnp.zeros_like(grid)
    barrier = pltpu.get_barrier_semaphore()
    for count, where_to in ((inner, in_inner), (outer, in_outer), (depth, in_depth)):
        for o in range(1, count):
            pl.semaphore_signal(barrier, inc=1, device_id=where_to(o), device_id_type=MESH)
    pl.semaphore_wait(barrier, inner + outer + depth - 3)

    started = []

    def send(src, dst, ssem, rsem, to):
        copy = pltpu.make_async_remote_copy(
            src_ref=src, dst_ref=dst, send_sem=ssem, recv_sem=rsem, device_id=to, device_id_type=MESH
        )
        copy.start()
        started.append(copy)
        return copy

    for copy in fetched[:3]:
        copy.wait()
    table[...] = jnp.zeros_like(table)
    table[0:1, 0:4] = nb_ref[...]
    table[1:2, 0:4] = se_ref[...]
    table[2:3, 0:4] = fl_ref[...]
    tables[group] = table[...]
    table_copies = [
        send(table, tables.at[group], tab_send.at[o], tab_recv.at[o], in_outer(o)) for o in range(1, outer)
    ]

    pos = (lax.broadcasted_iota(jnp.int32, (8, WIDTH), 1) - LO).astype(jnp.float32)
    col = pos - NI * jnp.floor((pos + 0.5) * (1.0 / NI))
    inside = (pos > -0.5) & (pos < CELLS - 0.5)
    at_west = (col < 0.5) & inside
    at_east = (col > NI - 1.5) & inside
    on_edge = jnp.where(at_west | at_east, 1.0, 0.0)
    lane = lax.broadcasted_iota(jnp.int32, (total, LANES), 1)
    odd = lax.rem(lane, 2) == 1
    odd6 = lax.rem(lax.broadcasted_iota(jnp.int32, (6 * rows, LANES), 1), 2) == 1
    level = lax.broadcasted_iota(jnp.int32, (rows, CELLS), 0)
    level8 = lax.broadcasted_iota(jnp.int32, (rows, LANES), 0)
    tail = jnp.zeros((total, LANES), jnp.float32)
    for j in range(NJ - 64):
        for x in (NI * j % LANES, (NI * j + NI - 1) % LANES):
            tail = jnp.where(lane == x, 1.0, tail)

    r0 = lax.broadcasted_iota(jnp.int32, (LANES, LANES), 0)
    r1 = lax.broadcasted_iota(jnp.int32, (LANES, LANES), 1)
    rev_i = jnp.where(r0 + r1 == NI - 1, 1.0, 0.0)

    for copy in fetched[3:]:
        copy.wait()
    wet = jnp.broadcast_to(wet_ref[...].astype(jnp.float32), (rows, CELLS))
    mdif, tdif, mix = mdif_ref[0], tdif_ref[0], mix_ref[0]

    def running(x, down):
        k = 1
        while k < rows:
            if down:
                x = x + jnp.where(level >= k, roll(x, k, 0), 0.0)
            else:
                x = x + jnp.where(level < rows - k, roll(x, rows - k, 0), 0.0)
            k *= 2
        return x

    m, s, lm, lt = mom_ref[0], tra_ref[0], mcot_ref[0], tcot_ref[0]
    has_above = jnp.where(d > 0, 1.0, 0.0)
    has_below = jnp.where(d < depth - 1, 1.0, 0.0)
    weights = None

    for r in range(2):
        gath = (gath_0, gath_1)[r]
        mixed = mix * lt
        edge_copies = []
        if depth > 1:
            edge_s[r, 0, 0:1] = s[rows - 1 : rows]
            edge_s[r, 0, 1:2] = mixed[rows - 1 : rows]
            edge_s[r, 1, 0:1] = s[0:1]
            edge_s[r, 1, 1:2] = mixed[0:1]
            for i, o in ((0, 1), (1, depth - 1)):
                edge_copies.append(
                    send(edge_s.at[r, i], edge_r.at[r, i], e_send.at[r, i], e_recv.at[r, i], in_depth(o))
                )
        back = running(lm, False)
        u = tdif * lt + press * back
        w_m = mdif * lm
        t_sum = press * back[0:1]
        grid[0:rows, LO:HI] = wet * m
        grid[rows : 2 * rows, LO:HI] = wet * s
        grid[2 * rows : 3 * rows, LO:HI] = wet * w_m
        grid[3 * rows : 4 * rows, LO:HI] = wet * u
        grid[4 * rows : 5 * rows, LO:HI] = jnp.where(level == 0, wet, jnp.where(level == 1, wet * t_sum, 0.0))

        tail_at = WIDTH - 2 * LANES
        north = roll(grid[:, tail_at:WIDTH], -(HI - NI - tail_at))[:, :LANES]
        south = grid[:, LO : LO + LANES]
        last = None
        for g in range(5):
            span = slice(g * rows, (g + 1) * rows)
            packed = []
            for a, b in ((1, 1 + FIRST), (1 + FIRST, CHUNKS)):
                acc = None
                for v in range(a, b):
                    cut = slice(v * LANES, (v + 1) * LANES)
                    piece = grid[span, cut] * on_edge[:, cut]
                    acc = piece if acc is None else acc + piece
                packed.append(acc)
            last = packed[1] if g == 0 else last + roll(packed[1], 2 * g)
            if g < 4:
                gath[member, g] = north[span]
                gath[member, 4 + g] = south[span]
                gath[member, 8 + g] = packed[0]
            else:
                gath[member, 12] = jnp.where(level8 < 2, north[span], 0.0) + roll(
                    jnp.where(level8 < 2, south[span], 0.0), 2, 0
                ) + roll(packed[0], 4, 0)
        gath[member, 13] = last
        copies = [
            send(gath.at[member], gath.at[member], g_send.at[r, o], g_recv.at[r, o], in_inner(o))
            for o in range(1, inner)
        ]
        if r == 0:
            for copy in table_copies:
                copy.wait_recv()
            local = pltpu.make_async_copy(tables, tables_s, tab_local)
            local.start()
            local.wait()
        for copy in copies:
            copy.wait_recv()

        def strips_for(target):
            def source(direction):
                tile = tables_s[target, 0, direction]
                edge = tables_s[target, 1, direction]
                known = jnp.maximum(tile, 0)
                here = (tile >= 0) & (lax.div(known, inner) == group)
                return lax.rem(known, inner), edge, jnp.where(here, 1.0, 0.0)

            result = []
            odds = []
            for direction in range(2):
                tile, edge, here = source(direction)
                edge = jnp.where(edge == 0, 0, 1)
                result.append((gath[tile, pl.ds(4 * edge, 4)] * here).reshape(4 * rows, LANES))
                two = gath[tile, 12] * here
                second = edge.astype(jnp.float32)
                odds.append(roll(two, -2, 0) * second + two * (1.0 - second))
            east, east_edge, east_here = source(2)
            west, west_edge, west_here = source(3)
            east_turn = jnp.where(east_edge == 3, 1.0, 0.0)
            west_turn = jnp.where(west_edge == 2, 1.0, 0.0)
            e = gath[east, 8:14].reshape(6 * rows, LANES)
            e = (roll(e, NI - 1) * east_turn + e * (1.0 - east_turn)) * east_here
            w = gath[west, 8:14].reshape(6 * rows, LANES)
            w = (roll(w, 1 - NI) * west_turn + w * (1.0 - west_turn)) * west_here
            side = jnp.where(odd6, e, w)
            mid = side[4 * rows : 5 * rows]
            mid = jnp.where(level8 < 2, odds[0], jnp.where(level8 < 4, roll(odds[1], 2, 0), mid))
            return jnp.concatenate([result[0], result[1], side[: 4 * rows], mid, side[5 * rows :]], axis=0)

        copies = []
        for o in range(1, outer):
            part[r, o] = strips_for(lax.rem(group + o, outer)).reshape(14, rows, LANES)
            copies.append(send(part.at[r, o], halo.at[r, o], h_send.at[r, o], h_recv.at[r, o], in_outer(o)))
        merged = strips_for(group)
        for o in range(1, outer):
            copies[o - 1].wait_recv()
            merged = merged + halo[r, o].reshape(14 * rows, LANES)
        mid, last = merged[12 * rows : 13 * rows], merged[13 * rows :]
        strips = [
            jnp.concatenate([merged[: 4 * rows], mid], axis=0),
            jnp.concatenate([merged[4 * rows : 8 * rows], roll(mid, -2, 0)], axis=0),
            jnp.concatenate([merged[8 * rows : 12 * rows], roll(mid, -4, 0)], axis=0),
            jnp.where(tail > 0.5, jnp.concatenate([roll(last, -2 * g) for g in range(5)], axis=0), 0.0),
        ]

        flip = [jnp.where(tables_s[group, 2, k] == 1, 1.0, 0.0) for k in range(4)]
        dot = functools.partial(jnp.dot, precision=EXACT, preferred_element_type=jnp.float32)
        north = dot(strips[0], rev_i) * flip[0] + strips[0] * (1.0 - flip[0])
        south = dot(strips[1], rev_i) * flip[1] + strips[1] * (1.0 - flip[1])
        both = lax.rem(r0, 2) == 0
        aim = jnp.where(both, NI * (NJ - 1) % LANES, (NI * (NJ - 1) + 2 * (NI - 1)) % LANES)
        turn = jnp.where(lax.rem(r0 + r1 + LANES * 4 - aim, LANES) == 0, 1.0, 0.0)
        one, two = dot(strips[2], turn), dot(strips[3], turn)
        turned_one = jnp.where(tail > 0.5, two, one)
        turned_two = jnp.where(tail > 0.5, one, 0.0)
        ew_flip = jnp.where(odd, flip[2], flip[3])
        ew_one = jnp.where(ew_flip > 0.5, turned_one, strips[2])
        ew_two = jnp.where(ew_flip > 0.5, turned_two, strips[3])

        grid[:, 0:LANES] = roll(south, LANES - NI)
        end = WIDTH - LANES
        grid[:, end:] = jnp.where(lane < HI - end, grid[:, end:], roll(north, HI - end))

        def around(g):
            span = slice(g * rows, (g + 1) * rows)
            x = grid[span, :]
            side = jnp.concatenate(
                [ew_one[span]] * (1 + FIRST) + [ew_two[span]] * (CHUNKS - 1 - FIRST), axis=1
            )
            east = jnp.where(at_east, side, roll(x, -1))
            west = jnp.where(at_west, side, roll(x, 1))
            return (roll(x, -NI) + roll(x, NI) + east + west)[:, LO:HI]

        extra = around(4)
        weights = extra[0:1]
        lap_t = wet[0:1] * (extra[1:2] - weights * t_sum)
        lap_s = wet * (around(1) - weights * s)
        sums = running(lap_s, True)
        copies = []
        if depth > 1:
            carry_s[r, 0:1] = sums[rows - 1 : rows]
            carry_s[r, 1:2] = lap_t
            copies = [
                send(carry_s.at[r], carry_r.at[r, o], c_send.at[r, o], c_recv.at[r, o], in_depth(o))
                for o in range(1, depth)
            ]
        lap_m = wet * (around(0) - weights * m)
        lap_w = wet * (around(2) - weights * w_m)
        lap_u = wet * (around(3) - weights * u)
        m_next = m + mdif * lap_m + press * sums
        lm_next = lm + lap_w + 0.2 * lt

        for copy in edge_copies:
            copy.wait_recv()

        def vertical(q, which):
            above, below = q[0:1], q[rows - 1 : rows]
            if depth > 1:
                above = edge_r[r, 0, which : which + 1] * has_above + above * (1.0 - has_above)
                below = edge_r[r, 1, which : which + 1] * has_below + below * (1.0 - has_below)
            up = jnp.where(level == 0, above, roll(q, 1, 0))
            down = jnp.where(level == rows - 1, below, roll(q, rows - 1, 0))
            return (up - q) + (down - q)

        s_next = s + tdif * lap_s + mix * vertical(s, 0) + 0.2 * m
        lt_next = lt + lap_u + vertical(mixed, 1)
        for o in range(1, depth):
            copies[o - 1].wait_recv()
            origin = lax.rem(d + depth - o, depth)
            m_next = m_next + carry_r[r, o, 0:1] * jnp.where(origin < d, press, 0.0)
            lt_next = lt_next + carry_r[r, o, 1:2] * jnp.where(origin > d, 1.0, 0.0)
        m, s, lm, lt = m_next, s_next, lm_next, lt_next

    mom_out[0] = m
    tra_out[0] = s
    mgrad_out[0] = lm
    tgrad_out[0] = lt
    for copy in started:
        copy.wait_send()


def write_out(*refs):
    sources, targets, staged, sems = refs[:4], refs[4:8], refs[8:12], refs[12]
    reads = [pltpu.make_async_copy(sources[k], staged[k], sems.at[0, k]) for k in range(4)]
    writes = [pltpu.make_async_copy(staged[k], targets[k], sems.at[1, k]) for k in range(4)]
    for copy in reads:
        copy.start()
    for read, write in zip(reads, writes):
        read.wait()
        write.start()
    for copy in writes:
        copy.wait()


def solution(mesh):
    tiles, depth = mesh.shape["tiles"], mesh.shape["depth"]
    inner = max(k for k in range(1, tiles + 1) if tiles % k == 0 and k * k <= tiles)
    outer = tiles // inner

    def local(*args):
        rows = args[0].shape[1]
        total = 5 * rows
        dma = pltpu.SemaphoreType.DMA
        f32 = jnp.float32
        shape = jax.ShapeDtypeStruct(args[0].shape, f32)
        vmem = pl.BlockSpec(memory_space=pltpu.VMEM)
        hbm = pl.BlockSpec(memory_space=pltpu.MemorySpace.HBM)
        results = pl.pallas_call(
            functools.partial(kernel, inner, outer, depth, rows * depth),
            out_shape=(shape,) * 4,
            in_specs=[hbm] * 11,
            out_specs=(vmem,) * 4,
            scratch_shapes=[
                *[pltpu.VMEM(a.shape, a.dtype) for a in args],
                pltpu.VMEM((8, LANES), jnp.int32),
                pltpu.VMEM((outer, 8, LANES), jnp.int32),
                pltpu.SMEM((outer, 8, LANES), jnp.int32),
                pltpu.VMEM((total, WIDTH), f32),
                pltpu.VMEM((inner, 14, rows, LANES), f32),
                pltpu.VMEM((inner, 14, rows, LANES), f32),
                pltpu.VMEM((2, outer, 14, rows, LANES), f32),
                pltpu.VMEM((2, outer, 14, rows, LANES), f32),
                pltpu.VMEM((2, 2, 2, CELLS), f32),
                pltpu.VMEM((2, 2, 2, CELLS), f32),
                pltpu.VMEM((2, 2, CELLS), f32),
                pltpu.VMEM((2, depth, 2, CELLS), f32),
                dma((11,)), dma((outer,)), dma((outer,)), dma(()),
                dma((2, inner)), dma((2, inner)),
                dma((2, outer)), dma((2, outer)),
                dma((2, 2)), dma((2, 2)),
                dma((2, depth)), dma((2, depth)),
            ],
            compiler_params=pltpu.CompilerParams(
                collective_id=0, has_side_effects=True, vmem_limit_bytes=62 * 1024 * 1024
            ),
        )(*args)
        return pl.pallas_call(
            write_out,
            out_shape=(shape,) * 4,
            in_specs=[pl.BlockSpec(memory_space=pl.ANY)] * 4,
            out_specs=(hbm,) * 4,
            scratch_shapes=[pltpu.VMEM(shape.shape, f32)] * 4 + [dma((2, 4))],
            compiler_params=pltpu.CompilerParams(vmem_limit_bytes=62 * 1024 * 1024),
        )(*results)

    whole = P("tiles", "depth", None)
    flat = P("tiles", None)
    in_specs = (whole,) * 5 + (flat,) * 4 + (whole,) * 2
    return jax.shard_map(local, mesh=mesh, in_specs=in_specs, out_specs=(whole,) * 4, check_vma=False)
```

```python
import functools

import jax
import jax.numpy as jnp
from jax import lax
from jax.experimental import pallas as pl
from jax.experimental.pallas import tpu as pltpu
from jax.sharding import PartitionSpec as P

NI = 90
NJ = 70
CELLS = NI * NJ
LANES = 128
LO = LANES
HI = LANES + CELLS
WIDTH = -(-(HI + NI) // LANES) * LANES
CHUNKS = WIDTH // LANES
FIRST = 64 * NI // LANES
MESH = pl.DeviceIdType.MESH
EXACT = lax.Precision.HIGHEST


def roll(x, shift, axis=1):
    return pltpu.roll(x, shift % x.shape[axis], axis)


def kernel(
    inner, outer, depth, levels_all,
    mom_hbm, tra_hbm, mdif_hbm, tdif_hbm, mix_hbm, wet_hbm, nb_hbm, se_hbm, fl_hbm, mcot_hbm, tcot_hbm,
    mom_out, tra_out, mgrad_out, tgrad_out,
    mom_ref, tra_ref, mdif_ref, tdif_ref, mix_ref, wet_ref, nb_ref, se_ref, fl_ref, mcot_ref, tcot_ref,
    table, tables, tables_s, grid, base, gath_0a, gath_0b, gath_1a, gath_1b, part, halo, edge_s, edge_r, carry_s, carry_r,
    in_sem, tab_send, tab_recv, tab_local, g_send, g_recv, h_send, h_recv, e_send, e_recv, c_send, c_recv,
):
    me = lax.axis_index("tiles")
    d = lax.axis_index("depth")
    member = lax.rem(me, inner)
    group = lax.div(me, inner)
    rows = mom_ref.shape[1]
    total = grid.shape[0]
    press = -0.1 * levels_all ** (-0.5)

    def in_inner(o):
        return {"tiles": group * inner + lax.rem(member + o, inner), "depth": d}

    def in_outer(o):
        return {"tiles": lax.rem(group + o, outer) * inner + member, "depth": d}

    def in_depth(o):
        return {"tiles": me, "depth": lax.rem(d + o, depth)}

    fetched = []
    for k, (src, dst) in enumerate((
        (nb_hbm, nb_ref), (se_hbm, se_ref), (fl_hbm, fl_ref), (wet_hbm, wet_ref), (mcot_hbm, mcot_ref),
        (tdif_hbm, tdif_ref), (tcot_hbm, tcot_ref), (tra_hbm, tra_ref), (mom_hbm, mom_ref), (mdif_hbm, mdif_ref),
        (mix_hbm, mix_ref),
    )):
        fetched.append(pltpu.make_async_copy(src, dst, in_sem.at[k]))
        fetched[-1].start()
    grid[...] = jnp.zeros_like(grid)
    barrier = pltpu.get_barrier_semaphore()
    for count, where_to in ((inner, in_inner), (outer, in_outer), (depth, in_depth)):
        for o in range(1, count):
            pl.semaphore_signal(barrier, inc=1, device_id=where_to(o), device_id_type=MESH)

    started = []

    def send(src, dst, ssem, rsem, to):
        copy = pltpu.make_async_remote_copy(
            src_ref=src, dst_ref=dst, send_sem=ssem, recv_sem=rsem, device_id=to, device_id_type=MESH
        )
        copy.start()
        started.append(copy)
        return copy

    for copy in fetched[:3]:
        copy.wait()
    table[...] = jnp.zeros_like(table)
    table[0:1, 0:4] = nb_ref[...]
    table[1:2, 0:4] = se_ref[...]
    table[2:3, 0:4] = fl_ref[...]
    tables[group] = table[...]
    pos = (lax.broadcasted_iota(jnp.int32, (8, WIDTH), 1) - LO).astype(jnp.float32)
    col = pos - NI * jnp.floor((pos + 0.5) * (1.0 / NI))
    inside = (pos > -0.5) & (pos < CELLS - 0.5)
    at_west = (col < 0.5) & inside
    at_east = (col > NI - 1.5) & inside
    on_edge = jnp.where(at_west | at_east, 1.0, 0.0)
    lane = lax.broadcasted_iota(jnp.int32, (total, LANES), 1)
    odd = lax.rem(lane, 2) == 1
    level = lax.broadcasted_iota(jnp.int32, (rows, CELLS), 0)
    level8 = lax.broadcasted_iota(jnp.int32, (rows, LANES), 0)
    tail = jnp.zeros((total, LANES), jnp.float32)
    for j in range(NJ - 64):
        for x in (NI * j % LANES, (NI * j + NI - 1) % LANES):
            tail = jnp.where(lane == x, 1.0, tail)

    r0 = lax.broadcasted_iota(jnp.int32, (LANES, LANES), 0)
    r1 = lax.broadcasted_iota(jnp.int32, (LANES, LANES), 1)
    rev_i = jnp.where(r0 + r1 == NI - 1, 1.0, 0.0)

    for copy in fetched[3:]:
        copy.wait()
    wet = jnp.broadcast_to(wet_ref[...].astype(jnp.float32), (rows, CELLS))
    mdif, tdif, mix = mdif_ref[0], tdif_ref[0], mix_ref[0]

    def running(x, down):
        k = 1
        while k < rows:
            if down:
                x = x + jnp.where(level >= k, roll(x, k, 0), 0.0)
            else:
                x = x + jnp.where(level < rows - k, roll(x, rows - k, 0), 0.0)
            k *= 2
        return x

    m, s, lm, lt = mom_ref[0], tra_ref[0], mcot_ref[0], tcot_ref[0]
    has_above = jnp.where(d > 0, 1.0, 0.0)
    has_below = jnp.where(d < depth - 1, 1.0, 0.0)

    for r in range(2):
        gath_a, gath_b = ((gath_0a, gath_0b), (gath_1a, gath_1b))[r]
        mixed = mix * lt
        back = running(lm, False)
        u = tdif * lt + press * back
        w_m = mdif * lm
        t_sum = press * back[0:1]
        grid[0:rows, LO:HI] = wet * m
        grid[rows : 2 * rows, LO:HI] = wet * s
        grid[2 * rows : 3 * rows, LO:HI] = jnp.where(level == 0, wet, jnp.where(level == 1, wet * t_sum, 0.0))
        grid[3 * rows : 4 * rows, LO:HI] = wet * w_m
        grid[4 * rows : 5 * rows, LO:HI] = wet * u

        tail_at = WIDTH - 2 * LANES
        north = roll(grid[:, tail_at:WIDTH], -(HI - NI - tail_at))[:, :LANES]
        south = grid[:, LO : LO + LANES]
        last = None
        for g in range(5):
            span = slice(g * rows, (g + 1) * rows)
            packed = []
            for a, b in ((1, 1 + FIRST), (1 + FIRST, CHUNKS)):
                acc = None
                for v in range(a, b):
                    cut = slice(v * LANES, (v + 1) * LANES)
                    piece = grid[span, cut] * on_edge[:, cut]
                    acc = piece if acc is None else acc + piece
                packed.append(acc)
            last = packed[1] if g == 0 else last + roll(packed[1], 2 * g)
            if g == 2:
                gath_a[member, 6] = jnp.where(level8 < 2, north[span], 0.0) + roll(
                    jnp.where(level8 < 2, south[span], 0.0), 2, 0
                ) + roll(packed[0], 4, 0)
            else:
                gath, k = (gath_a, g) if g < 2 else (gath_b, g - 3)
                gath[member, k] = north[span]
                gath[member, 2 + k] = south[span]
                gath[member, 4 + k] = packed[0]
        gath_a[member, 7] = last

        if r == 0:
            pl.semaphore_wait(barrier, inner + outer + depth - 3)
            table_copies = [
                send(table, tables.at[group], tab_send.at[o], tab_recv.at[o], in_outer(o)) for o in range(1, outer)
            ]
        first_copies = [
            [
                send(gath.at[member], gath.at[member], g_send.at[r, h, o], g_recv.at[r, h, o], in_inner(o))
                for o in range(1, inner)
            ]
            for h, gath in enumerate((gath_a, gath_b))
        ]
        edge_copies = []
        if depth > 1:
            edge_s[r, 0, 0:1] = s[rows - 1 : rows]
            edge_s[r, 0, 1:2] = mixed[rows - 1 : rows]
            edge_s[r, 1, 0:1] = s[0:1]
            edge_s[r, 1, 1:2] = mixed[0:1]
            for i, o in ((0, 1), (1, depth - 1)):
                edge_copies.append(
                    send(edge_s.at[r, i], edge_r.at[r, i], e_send.at[r, i], e_recv.at[r, i], in_depth(o))
                )

        def inside_sums(g):
            span = slice(g * rows, (g + 1) * rows)
            x = grid[span, :]
            east = jnp.where(at_east, 0.0, roll(x, -1))
            west = jnp.where(at_west, 0.0, roll(x, 1))
            base[span, :] = roll(x, -NI) + roll(x, NI) + east + west

        inside_sums(0)
        inside_sums(1)
        if r == 0:
            for copy in table_copies:
                copy.wait_recv()
            local = pltpu.make_async_copy(tables, tables_s, tab_local)
            local.start()
            local.wait()

        def strips_for(target, h):
            gath = (gath_a, gath_b)[h]

            def source(direction):
                tile = tables_s[target, 0, direction]
                edge = tables_s[target, 1, direction]
                known = jnp.maximum(tile, 0)
                here = (tile >= 0) & (lax.div(known, inner) == group)
                return lax.rem(known, inner), edge, jnp.where(here, 1.0, 0.0)

            result = []
            odds = []
            for direction in range(2):
                tile, edge, here = source(direction)
                edge = jnp.where(edge == 0, 0, 1)
                result.append((gath[tile, pl.ds(2 * edge, 2)] * here).reshape(2 * rows, LANES))
                if h == 0:
                    two = gath[tile, 6] * here
                    second = edge.astype(jnp.float32)
                    odds.append(roll(two, -2, 0) * second + two * (1.0 - second))
            east, east_edge, east_here = source(2)
            west, west_edge, west_here = source(3)
            east_turn = jnp.where(east_edge == 3, 1.0, 0.0)
            west_turn = jnp.where(west_edge == 2, 1.0, 0.0)
            size = gath.shape[1] - 4
            e = gath[east, 4:].reshape(size * rows, LANES)
            e = (roll(e, NI - 1) * east_turn + e * (1.0 - east_turn)) * east_here
            w = gath[west, 4:].reshape(size * rows, LANES)
            w = (roll(w, 1 - NI) * west_turn + w * (1.0 - west_turn)) * west_here
            side = jnp.where(odd[: size * rows], e, w)
            if h == 0:
                mid = side[2 * rows : 3 * rows]
                mid = jnp.where(level8 < 2, odds[0], jnp.where(level8 < 4, roll(odds[1], 2, 0), mid))
                side = jnp.concatenate([side[: 2 * rows], mid, side[3 * rows :]], axis=0)
            return jnp.concatenate(result + [side], axis=0)

        spots = (slice(0, 8), slice(8, 14))
        second_copies = []
        for h in range(2):
            for copy in first_copies[h]:
                copy.wait_recv()
            copies = []
            for o in range(1, outer):
                strips = strips_for(lax.rem(group + o, outer), h)
                part[r, o, spots[h]] = strips.reshape(strips.shape[0] // rows, rows, LANES)
                copies.append(
                    send(
                        part.at[r, o, spots[h]], halo.at[r, o, spots[h]],
                        h_send.at[r, h, o], h_recv.at[r, h, o], in_outer(o),
                    )
                )
            second_copies.append(copies)
        mine = [strips_for(group, h) for h in range(2)]
        for g in (2, 3, 4):
            inside_sums(g)

        for copy in edge_copies:
            copy.wait_recv()

        def vertical(q, which):
            above, below = q[0:1], q[rows - 1 : rows]
            if depth > 1:
                above = edge_r[r, 0, which : which + 1] * has_above + above * (1.0 - has_above)
                below = edge_r[r, 1, which : which + 1] * has_below + below * (1.0 - has_below)
            up = jnp.where(level == 0, above, roll(q, 1, 0))
            down = jnp.where(level == rows - 1, below, roll(q, rows - 1, 0))
            return (up - q) + (down - q)

        s_next = s + mix * vertical(s, 0) + 0.2 * m
        lt_next = lt + vertical(mixed, 1)
        lm_next = lm + 0.2 * lt

        flip = [jnp.where(tables_s[group, 2, k] == 1, 1.0, 0.0) for k in range(4)]
        dot = functools.partial(jnp.dot, precision=EXACT, preferred_element_type=jnp.float32)
        both = lax.rem(r0, 2) == 0
        aim = jnp.where(both, NI * (NJ - 1) % LANES, (NI * (NJ - 1) + 2 * (NI - 1)) % LANES)
        turn = jnp.where(lax.rem(r0 + r1 + LANES * 4 - aim, LANES) == 0, 1.0, 0.0)

        def receive(h):
            merged = mine[h]
            for o in range(1, outer):
                second_copies[h][o - 1].wait_recv()
                merged = merged + halo[r, o, spots[h]].reshape(merged.shape)
            return merged

        def close(strips, lo):
            count = strips[0].shape[0]
            here, own, parity = slice(lo, lo + count), lane[:count], odd[:count]
            ends = tail[:count] > 0.5
            north = dot(strips[0], rev_i) * flip[0] + strips[0] * (1.0 - flip[0])
            south = dot(strips[1], rev_i) * flip[1] + strips[1] * (1.0 - flip[1])
            one, two = dot(strips[2], turn), dot(strips[3], turn)
            ew_flip = jnp.where(parity, flip[2], flip[3]) > 0.5
            ew_one = jnp.where(ew_flip, jnp.where(ends, two, one), strips[2])
            ew_two = jnp.where(ew_flip, jnp.where(ends, one, 0.0), strips[3])
            base[here, LO : LO + LANES] = base[here, LO : LO + LANES] + jnp.where(own < NI, south, 0.0)
            north = jnp.concatenate([jnp.where(own < NI, north, 0.0), jnp.zeros_like(north)], axis=1)
            base[here, tail_at:] = base[here, tail_at:] + roll(north, HI - NI - tail_at)
            return ew_one, ew_two

        def around(g, lo, sides):
            span = slice(g * rows - lo, (g + 1) * rows - lo)
            side = jnp.concatenate(
                [sides[0][span]] * (1 + FIRST) + [sides[1][span]] * (CHUNKS - 1 - FIRST), axis=1
            )
            return (base[g * rows : (g + 1) * rows, :] + side * on_edge)[:, LO:HI]

        got = receive(0)
        mid, last = got[6 * rows : 7 * rows], got[7 * rows :]
        tails = [roll(last, -2 * g) for g in range(5)]
        lo = 3 * rows
        sides = close([
            jnp.concatenate([got[: 2 * rows], mid], axis=0),
            jnp.concatenate([got[2 * rows : 4 * rows], roll(mid, -2, 0)], axis=0),
            jnp.concatenate([got[4 * rows : 6 * rows], roll(mid, -4, 0)], axis=0),
            jnp.where(tail[:lo] > 0.5, jnp.concatenate(tails[:3], axis=0), 0.0),
        ], 0)
        extra = around(2, 0, sides)
        weights = extra[0:1]
        lap_t = wet[0:1] * (extra[1:2] - weights * t_sum)
        lap_s = wet * (around(1, 0, sides) - weights * s)
        sums = running(lap_s, True)
        copies = []
        if depth > 1:
            carry_s[r, 0:1] = sums[rows - 1 : rows]
            carry_s[r, 1:2] = lap_t
            copies = [
                send(carry_s.at[r], carry_r.at[r, o], c_send.at[r, o], c_recv.at[r, o], in_depth(o))
                for o in range(1, depth)
            ]
        m_next = m + mdif * (wet * (around(0, 0, sides) - weights * m)) + press * sums
        s_next = s_next + tdif * lap_s

        got = receive(1)
        sides = close([
            got[: 2 * rows],
            got[2 * rows : 4 * rows],
            got[4 * rows :],
            jnp.where(tail[: 2 * rows] > 0.5, jnp.concatenate(tails[3:], axis=0), 0.0),
        ], lo)
        lm_next = lm_next + wet * (around(3, lo, sides) - weights * w_m)
        lt_next = lt_next + wet * (around(4, lo, sides) - weights * u)
        for o in range(1, depth):
            copies[o - 1].wait_recv()
            origin = lax.rem(d + depth - o, depth)
            m_next = m_next + carry_r[r, o, 0:1] * jnp.where(origin < d, press, 0.0)
            lt_next = lt_next + carry_r[r, o, 1:2] * jnp.where(origin > d, 1.0, 0.0)
        m, s, lm, lt = m_next, s_next, lm_next, lt_next

    mom_out[0] = m
    tra_out[0] = s
    mgrad_out[0] = lm
    tgrad_out[0] = lt
    for copy in started:
        copy.wait_send()


def write_out(*refs):
    sources, targets, staged, sems = refs[:4], refs[4:8], refs[8:12], refs[12]
    reads = [pltpu.make_async_copy(sources[k], staged[k], sems.at[0, k]) for k in range(4)]
    writes = [pltpu.make_async_copy(staged[k], targets[k], sems.at[1, k]) for k in range(4)]
    for copy in reads:
        copy.start()
    for read, write in zip(reads, writes):
        read.wait()
        write.start()
    for copy in writes:
        copy.wait()


def solution(mesh):
    tiles, depth = mesh.shape["tiles"], mesh.shape["depth"]
    inner = max(k for k in range(1, tiles + 1) if tiles % k == 0 and k * k <= tiles)
    outer = tiles // inner

    def local(*args):
        rows = args[0].shape[1]
        total = 5 * rows
        dma = pltpu.SemaphoreType.DMA
        f32 = jnp.float32
        shape = jax.ShapeDtypeStruct(args[0].shape, f32)
        vmem = pl.BlockSpec(memory_space=pltpu.VMEM)
        hbm = pl.BlockSpec(memory_space=pltpu.MemorySpace.HBM)
        results = pl.pallas_call(
            functools.partial(kernel, inner, outer, depth, rows * depth),
            out_shape=(shape,) * 4,
            in_specs=[hbm] * 11,
            out_specs=(vmem,) * 4,
            scratch_shapes=[
                *[pltpu.VMEM(a.shape, a.dtype) for a in args],
                pltpu.VMEM((8, LANES), jnp.int32),
                pltpu.VMEM((outer, 8, LANES), jnp.int32),
                pltpu.SMEM((outer, 8, LANES), jnp.int32),
                pltpu.VMEM((total, WIDTH), f32),
                pltpu.VMEM((total, WIDTH), f32),
                pltpu.VMEM((inner, 8, rows, LANES), f32),
                pltpu.VMEM((inner, 6, rows, LANES), f32),
                pltpu.VMEM((inner, 8, rows, LANES), f32),
                pltpu.VMEM((inner, 6, rows, LANES), f32),
                pltpu.VMEM((2, outer, 14, rows, LANES), f32),
                pltpu.VMEM((2, outer, 14, rows, LANES), f32),
                pltpu.VMEM((2, 2, 2, CELLS), f32),
                pltpu.VMEM((2, 2, 2, CELLS), f32),
                pltpu.VMEM((2, 2, CELLS), f32),
                pltpu.VMEM((2, depth, 2, CELLS), f32),
                dma((11,)), dma((outer,)), dma((outer,)), dma(()),
                dma((2, 2, inner)), dma((2, 2, inner)),
                dma((2, 2, outer)), dma((2, 2, outer)),
                dma((2, 2)), dma((2, 2)),
                dma((2, depth)), dma((2, depth)),
            ],
            compiler_params=pltpu.CompilerParams(
                collective_id=0, has_side_effects=True, vmem_limit_bytes=62 * 1024 * 1024
            ),
        )(*args)
        return pl.pallas_call(
            write_out,
            out_shape=(shape,) * 4,
            in_specs=[pl.BlockSpec(memory_space=pl.ANY)] * 4,
            out_specs=(hbm,) * 4,
            scratch_shapes=[pltpu.VMEM(shape.shape, f32)] * 4 + [dma((2, 4))],
            compiler_params=pltpu.CompilerParams(vmem_limit_bytes=62 * 1024 * 1024),
        )(*results)

    whole = P("tiles", "depth", None)
    flat = P("tiles", None)
    in_specs = (whole,) * 5 + (flat,) * 4 + (whole,) * 2
    return jax.shard_map(local, mesh=mesh, in_specs=in_specs, out_specs=(whole,) * 4, check_vma=False)
```

```python
import functools

import jax
import jax.numpy as jnp
from jax import lax
from jax.experimental import pallas as pl
from jax.experimental.pallas import tpu as pltpu
from jax.sharding import PartitionSpec as P

NI = 90
NJ = 70
CELLS = NI * NJ
LANES = 128
LO = LANES
HI = LANES + CELLS
WIDTH = -(-(HI + NI) // LANES) * LANES
CHUNKS = WIDTH // LANES
FIRST = 64 * NI // LANES
MESH = pl.DeviceIdType.MESH
EXACT = lax.Precision.HIGHEST


def roll(x, shift, axis=1):
    return pltpu.roll(x, shift % x.shape[axis], axis)


def kernel(
    inner, outer, depth, levels_all,
    mom_hbm, tra_hbm, mdif_hbm, tdif_hbm, mix_hbm, wet_hbm, nb_hbm, se_hbm, fl_hbm, mcot_hbm, tcot_hbm,
    mom_out, tra_out, mgrad_out, tgrad_out,
    mom_ref, tra_ref, mdif_ref, tdif_ref, mix_ref, wet_ref, nb_ref, se_ref, fl_ref, mcot_ref, tcot_ref,
    table, tables, tables_s, grid, base, gath_0a, gath_0b, gath_1a, gath_1b, part, halo, edge_s, edge_r, carry_s, carry_r,
    in_sem, tab_send, tab_recv, tab_local, g_send, g_recv, h_send, h_recv, e_send, e_recv, c_send, c_recv,
):
    me = lax.axis_index("tiles")
    d = lax.axis_index("depth")
    member = lax.rem(me, inner)
    group = lax.div(me, inner)
    rows = mom_ref.shape[1]
    total = grid.shape[0]
    press = -0.1 * levels_all ** (-0.5)

    def in_inner(o):
        return {"tiles": group * inner + lax.rem(member + o, inner), "depth": d}

    def in_outer(o):
        return {"tiles": lax.rem(group + o, outer) * inner + member, "depth": d}

    def in_depth(o):
        return {"tiles": me, "depth": lax.rem(d + o, depth)}

    fetched = []
    for k, (src, dst) in enumerate((
        (nb_hbm, nb_ref), (se_hbm, se_ref), (fl_hbm, fl_ref), (wet_hbm, wet_ref), (mcot_hbm, mcot_ref),
        (tdif_hbm, tdif_ref), (tcot_hbm, tcot_ref), (tra_hbm, tra_ref), (mom_hbm, mom_ref), (mdif_hbm, mdif_ref),
        (mix_hbm, mix_ref),
    )):
        fetched.append(pltpu.make_async_copy(src, dst, in_sem.at[k]))
        fetched[-1].start()
    grid[...] = jnp.zeros_like(grid)
    barrier = pltpu.get_barrier_semaphore()
    for count, where_to in ((inner, in_inner), (outer, in_outer), (depth, in_depth)):
        for o in range(1, count):
            pl.semaphore_signal(barrier, inc=1, device_id=where_to(o), device_id_type=MESH)

    started = []

    def send(src, dst, ssem, rsem, to):
        copy = pltpu.make_async_remote_copy(
            src_ref=src, dst_ref=dst, send_sem=ssem, recv_sem=rsem, device_id=to, device_id_type=MESH
        )
        copy.start()
        started.append(copy)
        return copy

    for copy in fetched[:3]:
        copy.wait()
    table[...] = jnp.zeros_like(table)
    table[0:1, 0:4] = nb_ref[...]
    table[1:2, 0:4] = se_ref[...]
    table[2:3, 0:4] = fl_ref[...]
    tables[group] = table[...]
    pos = (lax.broadcasted_iota(jnp.int32, (8, WIDTH), 1) - LO).astype(jnp.float32)
    col = pos - NI * jnp.floor((pos + 0.5) * (1.0 / NI))
    inside = (pos > -0.5) & (pos < CELLS - 0.5)
    at_west = (col < 0.5) & inside
    at_east = (col > NI - 1.5) & inside
    on_edge = jnp.where(at_west | at_east, 1.0, 0.0)
    lane = lax.broadcasted_iota(jnp.int32, (total, LANES), 1)
    odd = lax.rem(lane, 2) == 1
    level = lax.broadcasted_iota(jnp.int32, (rows, CELLS), 0)
    level8 = lax.broadcasted_iota(jnp.int32, (rows, LANES), 0)
    tail = jnp.zeros((total, LANES), jnp.float32)
    for j in range(NJ - 64):
        for x in (NI * j % LANES, (NI * j + NI - 1) % LANES):
            tail = jnp.where(lane == x, 1.0, tail)

    r0 = lax.broadcasted_iota(jnp.int32, (LANES, LANES), 0)
    r1 = lax.broadcasted_iota(jnp.int32, (LANES, LANES), 1)
    rev_i = jnp.where(r0 + r1 == NI - 1, 1.0, 0.0)

    for copy in fetched[3:]:
        copy.wait()
    wet = jnp.broadcast_to(wet_ref[...].astype(jnp.float32), (rows, CELLS))
    mdif, tdif, mix = mdif_ref[0], tdif_ref[0], mix_ref[0]

    def running(x, down):
        k = 1
        while k < rows:
            if down:
                x = x + jnp.where(level >= k, roll(x, k, 0), 0.0)
            else:
                x = x + jnp.where(level < rows - k, roll(x, rows - k, 0), 0.0)
            k *= 2
        return x

    m, s, lm, lt = mom_ref[0], tra_ref[0], mcot_ref[0], tcot_ref[0]
    has_above = jnp.where(d > 0, 1.0, 0.0)
    has_below = jnp.where(d < depth - 1, 1.0, 0.0)

    for r in range(2):
        gath_a, gath_b = ((gath_0a, gath_0b), (gath_1a, gath_1b))[r]
        mixed = mix * lt
        back = running(lm, False)
        u = tdif * lt + press * back
        w_m = mdif * lm
        t_sum = press * back[0:1]
        grid[0:rows, LO:HI] = wet * m
        grid[rows : 2 * rows, LO:HI] = wet * s
        grid[2 * rows : 3 * rows, LO:HI] = jnp.where(level == 0, wet, jnp.where(level == 1, wet * t_sum, 0.0))
        grid[3 * rows : 4 * rows, LO:HI] = wet * w_m
        grid[4 * rows : 5 * rows, LO:HI] = wet * u

        tail_at = WIDTH - 2 * LANES
        north = roll(grid[:, tail_at:WIDTH], -(HI - NI - tail_at))[:, :LANES]
        south = grid[:, LO : LO + LANES]
        last = None
        for g in range(5):
            span = slice(g * rows, (g + 1) * rows)
            packed = []
            for a, b in ((1, 1 + FIRST), (1 + FIRST, CHUNKS)):
                acc = None
                for v in range(a, b):
                    cut = slice(v * LANES, (v + 1) * LANES)
                    piece = grid[span, cut] * on_edge[:, cut]
                    acc = piece if acc is None else acc + piece
                packed.append(acc)
            last = packed[1] if g == 0 else last + roll(packed[1], 2 * g)
            if g == 2:
                gath_a[member, 6] = jnp.where(level8 < 2, north[span], 0.0) + roll(
                    jnp.where(level8 < 2, south[span], 0.0), 2, 0
                ) + roll(packed[0], 4, 0)
            else:
                gath, k = (gath_a, g) if g < 2 else (gath_b, g - 3)
                gath[member, k] = north[span]
                gath[member, 2 + k] = south[span]
                gath[member, 4 + k] = packed[0]
        gath_a[member, 7] = last

        if r == 0:
            pl.semaphore_wait(barrier, inner + outer + depth - 3)
            table_copies = [
                send(table, tables.at[group], tab_send.at[o], tab_recv.at[o], in_outer(o)) for o in range(1, outer)
            ]
        first_copies = [
            [
                send(gath.at[member], gath.at[member], g_send.at[r, h, o], g_recv.at[r, h, o], in_inner(o))
                for o in range(1, inner)
            ]
            for h, gath in enumerate((gath_a, gath_b))
        ]
        edge_copies = []
        if depth > 1:
            edge_s[r, 0, 0:1] = s[rows - 1 : rows]
            edge_s[r, 0, 1:2] = mixed[rows - 1 : rows]
            edge_s[r, 1, 0:1] = s[0:1]
            edge_s[r, 1, 1:2] = mixed[0:1]
            for i, o in ((0, 1), (1, depth - 1)):
                edge_copies.append(
                    send(edge_s.at[r, i], edge_r.at[r, i], e_send.at[r, i], e_recv.at[r, i], in_depth(o))
                )

        def inside_sums(g):
            span = slice(g * rows, (g + 1) * rows)
            x = grid[span, :]
            east = jnp.where(at_east, 0.0, roll(x, -1))
            west = jnp.where(at_west, 0.0, roll(x, 1))
            base[span, :] = roll(x, -NI) + roll(x, NI) + east + west

        inside_sums(0)
        inside_sums(1)
        if r == 0:
            for copy in table_copies:
                copy.wait_recv()
            local = pltpu.make_async_copy(tables, tables_s, tab_local)
            local.start()
            local.wait()

        def strips_for(target, h):
            gath = (gath_a, gath_b)[h]

            def source(direction):
                tile = tables_s[target, 0, direction]
                edge = tables_s[target, 1, direction]
                known = jnp.maximum(tile, 0)
                here = (tile >= 0) & (lax.div(known, inner) == group)
                return lax.rem(known, inner), edge, jnp.where(here, 1.0, 0.0)

            result = []
            odds = []
            for direction in range(2):
                tile, edge, here = source(direction)
                edge = jnp.where(edge == 0, 0, 1)
                result.append((gath[tile, pl.ds(2 * edge, 2)] * here).reshape(2 * rows, LANES))
                if h == 0:
                    two = gath[tile, 6] * here
                    second = edge.astype(jnp.float32)
                    odds.append(roll(two, -2, 0) * second + two * (1.0 - second))
            east, east_edge, east_here = source(2)
            west, west_edge, west_here = source(3)
            east_turn = jnp.where(east_edge == 3, 1.0, 0.0)
            west_turn = jnp.where(west_edge == 2, 1.0, 0.0)
            size = gath.shape[1] - 4
            e = gath[east, 4:].reshape(size * rows, LANES)
            e = (roll(e, NI - 1) * east_turn + e * (1.0 - east_turn)) * east_here
            w = gath[west, 4:].reshape(size * rows, LANES)
            w = (roll(w, 1 - NI) * west_turn + w * (1.0 - west_turn)) * west_here
            side = jnp.where(odd[: size * rows], e, w)
            if h == 0:
                mid = side[2 * rows : 3 * rows]
                mid = jnp.where(level8 < 2, odds[0], jnp.where(level8 < 4, roll(odds[1], 2, 0), mid))
                side = jnp.concatenate([side[: 2 * rows], mid, side[3 * rows :]], axis=0)
            return jnp.concatenate(result + [side], axis=0)

        spots = (slice(0, 8), slice(8, 14))
        second_copies = []
        for h in range(2):
            for copy in first_copies[h]:
                copy.wait_recv()
            copies = []
            for o in range(1, outer):
                strips = strips_for(lax.rem(group + o, outer), h)
                part[r, o, spots[h]] = strips.reshape(strips.shape[0] // rows, rows, LANES)
                copies.append(
                    send(
                        part.at[r, o, spots[h]], halo.at[r, o, spots[h]],
                        h_send.at[r, h, o], h_recv.at[r, h, o], in_outer(o),
                    )
                )
            second_copies.append(copies)
        mine = [strips_for(group, h) for h in range(2)]
        for g in (2, 3, 4):
            inside_sums(g)

        for copy in edge_copies:
            copy.wait_recv()

        def vertical(q, which):
            above, below = q[0:1], q[rows - 1 : rows]
            if depth > 1:
                above = edge_r[r, 0, which : which + 1] * has_above + above * (1.0 - has_above)
                below = edge_r[r, 1, which : which + 1] * has_below + below * (1.0 - has_below)
            up = jnp.where(level == 0, above, roll(q, 1, 0))
            down = jnp.where(level == rows - 1, below, roll(q, rows - 1, 0))
            return (up - q) + (down - q)

        s_next = s + mix * vertical(s, 0) + 0.2 * m
        lt_next = lt + vertical(mixed, 1)
        lm_next = lm + 0.2 * lt

        flip = [jnp.where(tables_s[group, 2, k] == 1, 1.0, 0.0) for k in range(4)]
        dot = functools.partial(jnp.dot, precision=EXACT, preferred_element_type=jnp.float32)
        both = lax.rem(r0, 2) == 0
        aim = jnp.where(both, NI * (NJ - 1) % LANES, (NI * (NJ - 1) + 2 * (NI - 1)) % LANES)
        turn = jnp.where(lax.rem(r0 + r1 + LANES * 4 - aim, LANES) == 0, 1.0, 0.0)

        def receive(h):
            merged = mine[h]
            for o in range(1, outer):
                second_copies[h][o - 1].wait_recv()
                merged = merged + halo[r, o, spots[h]].reshape(merged.shape)
            return merged

        def close(strips, lo):
            count = strips[0].shape[0]
            here, own, parity = slice(lo, lo + count), lane[:count], odd[:count]
            ends = tail[:count] > 0.5
            turned = dot(jnp.concatenate(strips[:2], axis=0), rev_i)
            north = turned[:count] * flip[0] + strips[0] * (1.0 - flip[0])
            south = turned[count:] * flip[1] + strips[1] * (1.0 - flip[1])
            turned = dot(jnp.concatenate(strips[2:], axis=0), turn)
            one, two = turned[:count], turned[count:]
            ew_flip = jnp.where(parity, flip[2], flip[3]) > 0.5
            ew_one = jnp.where(ew_flip, jnp.where(ends, two, one), strips[2])
            ew_two = jnp.where(ew_flip, jnp.where(ends, one, 0.0), strips[3])
            base[here, LO : LO + LANES] = base[here, LO : LO + LANES] + jnp.where(own < NI, south, 0.0)
            north = jnp.concatenate([jnp.where(own < NI, north, 0.0), jnp.zeros_like(north)], axis=1)
            base[here, tail_at:] = base[here, tail_at:] + roll(north, HI - NI - tail_at)
            return ew_one, ew_two

        def around(g, lo, sides):
            span = slice(g * rows - lo, (g + 1) * rows - lo)
            side = jnp.concatenate(
                [sides[0][span]] * (1 + FIRST) + [sides[1][span]] * (CHUNKS - 1 - FIRST), axis=1
            )
            return (base[g * rows : (g + 1) * rows, :] + side * on_edge)[:, LO:HI]

        got = receive(0)
        mid, last = got[6 * rows : 7 * rows], got[7 * rows :]
        tails = [roll(last, -2 * g) for g in range(5)]
        lo = 3 * rows
        sides = close([
            jnp.concatenate([got[: 2 * rows], mid], axis=0),
            jnp.concatenate([got[2 * rows : 4 * rows], roll(mid, -2, 0)], axis=0),
            jnp.concatenate([got[4 * rows : 6 * rows], roll(mid, -4, 0)], axis=0),
            jnp.where(tail[:lo] > 0.5, jnp.concatenate(tails[:3], axis=0), 0.0),
        ], 0)
        extra = around(2, 0, sides)
        weights = extra[0:1]
        lap_t = wet[0:1] * (extra[1:2] - weights * t_sum)
        lap_s = wet * (around(1, 0, sides) - weights * s)
        sums = running(lap_s, True)
        copies = []
        if depth > 1:
            carry_s[r, 0:1] = sums[rows - 1 : rows]
            carry_s[r, 1:2] = lap_t
            copies = [
                send(carry_s.at[r], carry_r.at[r, o], c_send.at[r, o], c_recv.at[r, o], in_depth(o))
                for o in range(1, depth)
            ]
        m_next = m + mdif * (wet * (around(0, 0, sides) - weights * m)) + press * sums
        s_next = s_next + tdif * lap_s

        got = receive(1)
        sides = close([
            got[: 2 * rows],
            got[2 * rows : 4 * rows],
            got[4 * rows :],
            jnp.where(tail[: 2 * rows] > 0.5, jnp.concatenate(tails[3:], axis=0), 0.0),
        ], lo)
        lm_next = lm_next + wet * (around(3, lo, sides) - weights * w_m)
        lt_next = lt_next + wet * (around(4, lo, sides) - weights * u)
        for o in range(1, depth):
            copies[o - 1].wait_recv()
            origin = lax.rem(d + depth - o, depth)
            m_next = m_next + carry_r[r, o, 0:1] * jnp.where(origin < d, press, 0.0)
            lt_next = lt_next + carry_r[r, o, 1:2] * jnp.where(origin > d, 1.0, 0.0)
        m, s, lm, lt = m_next, s_next, lm_next, lt_next

    mom_out[0] = m
    tra_out[0] = s
    mgrad_out[0] = lm
    tgrad_out[0] = lt
    for copy in started:
        copy.wait_send()


def write_out(*refs):
    sources, targets, staged, sems = refs[:4], refs[4:8], refs[8:12], refs[12]
    reads = [pltpu.make_async_copy(sources[k], staged[k], sems.at[0, k]) for k in range(4)]
    writes = [pltpu.make_async_copy(staged[k], targets[k], sems.at[1, k]) for k in range(4)]
    for copy in reads:
        copy.start()
    for read, write in zip(reads, writes):
        read.wait()
        write.start()
    for copy in writes:
        copy.wait()


def solution(mesh):
    tiles, depth = mesh.shape["tiles"], mesh.shape["depth"]
    inner = max(k for k in range(1, tiles + 1) if tiles % k == 0 and k * k <= tiles)
    outer = tiles // inner

    def local(*args):
        rows = args[0].shape[1]
        total = 5 * rows
        dma = pltpu.SemaphoreType.DMA
        f32 = jnp.float32
        shape = jax.ShapeDtypeStruct(args[0].shape, f32)
        vmem = pl.BlockSpec(memory_space=pltpu.VMEM)
        hbm = pl.BlockSpec(memory_space=pltpu.MemorySpace.HBM)
        results = pl.pallas_call(
            functools.partial(kernel, inner, outer, depth, rows * depth),
            out_shape=(shape,) * 4,
            in_specs=[hbm] * 11,
            out_specs=(vmem,) * 4,
            scratch_shapes=[
                *[pltpu.VMEM(a.shape, a.dtype) for a in args],
                pltpu.VMEM((8, LANES), jnp.int32),
                pltpu.VMEM((outer, 8, LANES), jnp.int32),
                pltpu.SMEM((outer, 8, LANES), jnp.int32),
                pltpu.VMEM((total, WIDTH), f32),
                pltpu.VMEM((total, WIDTH), f32),
                pltpu.VMEM((inner, 8, rows, LANES), f32),
                pltpu.VMEM((inner, 6, rows, LANES), f32),
                pltpu.VMEM((inner, 8, rows, LANES), f32),
                pltpu.VMEM((inner, 6, rows, LANES), f32),
                pltpu.VMEM((2, outer, 14, rows, LANES), f32),
                pltpu.VMEM((2, outer, 14, rows, LANES), f32),
                pltpu.VMEM((2, 2, 2, CELLS), f32),
                pltpu.VMEM((2, 2, 2, CELLS), f32),
                pltpu.VMEM((2, 2, CELLS), f32),
                pltpu.VMEM((2, depth, 2, CELLS), f32),
                dma((11,)), dma((outer,)), dma((outer,)), dma(()),
                dma((2, 2, inner)), dma((2, 2, inner)),
                dma((2, 2, outer)), dma((2, 2, outer)),
                dma((2, 2)), dma((2, 2)),
                dma((2, depth)), dma((2, depth)),
            ],
            compiler_params=pltpu.CompilerParams(
                collective_id=0, has_side_effects=True, vmem_limit_bytes=62 * 1024 * 1024
            ),
        )(*args)
        return pl.pallas_call(
            write_out,
            out_shape=(shape,) * 4,
            in_specs=[pl.BlockSpec(memory_space=pl.ANY)] * 4,
            out_specs=(hbm,) * 4,
            scratch_shapes=[pltpu.VMEM(shape.shape, f32)] * 4 + [dma((2, 4))],
            compiler_params=pltpu.CompilerParams(vmem_limit_bytes=62 * 1024 * 1024),
        )(*results)

    whole = P("tiles", "depth", None)
    flat = P("tiles", None)
    in_specs = (whole,) * 5 + (flat,) * 4 + (whole,) * 2
    return jax.shard_map(local, mesh=mesh, in_specs=in_specs, out_specs=(whole,) * 4, check_vma=False)
```
